32 devices in a mesh: fsdp: 4 (over x, core), ctx: 2 (over y), tp: 4 (over z).
Axes of the slice: x: 2, y: 2, z: 4, core: 2. Of those that a mesh axis runs over, the one named last changes fastest.
Arguments:
- tokens: bfloat16 [16, 2048, 1152], P('fsdp', ('ctx', 'tp')), may hold values from -6 to 6
- picture: int32 [16, 2048], P('fsdp', 'ctx'), may hold values from 0 to 3, never falling along the last dimension, each value on 1 to 1024 neighbouring positions
- ln1_gain: float32 [1152], replicated, may hold values from 0.5 to 1.5
- ln1_bias: float32 [1152], replicated, may hold values from -1 to 1
- w_query: bfloat16 [1152, 1152], P('fsdp', 'tp'), may hold values from -0.1875 to 0.1875
- b_query: float32 [1152], replicated, may hold values from -1 to 1
- w_key: bfloat16 [1152, 1152], P('fsdp', 'tp'), may hold values from -0.1875 to 0.1875
- w_value: bfloat16 [1152, 1152], P('fsdp', 'tp'), may hold values from -0.1875 to 0.1875
- b_value: float32 [1152], replicated, may hold values from -1 to 1
- w_output: bfloat16 [1152, 1152], P('tp', 'fsdp'), may hold values from -4 to 4
- b_output: float32 [1152], replicated, may hold values from -1 to 1
- ln2_gain: float32 [1152], replicated, may hold values from 0.5 to 1.5
- ln2_bias: float32 [1152], replicated, may hold values from -1 to 1
- w_first: bfloat16 [1152, 4304], P('fsdp', 'tp'), may hold values from -0.1875 to 0.1875
- b_first: float32 [4304], replicated, may hold values from -1 to 1
- w_second: bfloat16 [4304, 1152], P('tp', 'fsdp'), may hold values from -0.09375 to 0.09375
- b_second: float32 [1152], replicated, may hold values from -1 to 1
- cotangent: bfloat16 [16, 2048, 1152], P('fsdp', ('ctx', 'tp')), may hold values from -6 to 6
Outputs:
- output: bfloat16 [16, 2048, 1152], P('fsdp', ('ctx', 'tp'))
- grad_tokens: float32 [16, 2048, 1152], P('fsdp', ('ctx', 'tp'))
- grad_ln1_gain: float32 [1152], replicated
- grad_ln1_bias: float32 [1152], replicated
- grad_w_query: float32 [1152, 1152], P(('fsdp', 'ctx'), 'tp')
- grad_b_query: float32 [1152], replicated
- grad_w_key: float32 [1152, 1152], P(('fsdp', 'ctx'), 'tp')
- grad_w_value: float32 [1152, 1152], P(('fsdp', 'ctx'), 'tp')
- grad_b_value: float32 [1152], replicated
- grad_w_output: float32 [1152, 1152], P('tp', ('fsdp', 'ctx'))
- grad_b_output: float32 [1152], replicated
- grad_ln2_gain: float32 [1152], replicated
- grad_ln2_bias: float32 [1152], replicated
- grad_w_first: float32 [1152, 4304], P(('fsdp', 'ctx'), 'tp')
- grad_b_first: float32 [4304], replicated
- grad_w_second: float32 [4304, 1152], P('tp', ('fsdp', 'ctx'))
- grad_b_second: float32 [1152], replicated
The draws below stay inside these ranges and needn't reach their ends.
Inputs may be any that keep to these rules, and one draw needn't show every extreme that they name: In each row picture numbers never fall along the 2048 tokens; each picture holds 1 to 1024 tokens and one holds exactly 1024.
All inputs are finite; a program needn't handle non-finite values.
Results may differ from the reference program's by a relative error of at most 0.02.
Values may be sent and summed in bfloat16 or wider, within the bound.
A program may use at most 512 MiB of HBM per device.

```python
import math
import jax
import jax.numpy as jnp
import numpy as np
from jax import lax

D = 1152
HEADS = 16
HD = 72
FF = 4304
SEQ = 2048
PICS = 4
MOST = 1024
ROWS = 16


def block_levels(rng, extent, shards, least, top_value):
    def one(position, parts):
        steps = jax.random.uniform(jax.random.fold_in(jax.random.fold_in(rng, 6), position), (parts,), jnp.float32, least / len(shards), top_value / len(shards))
        return jnp.repeat(jnp.exp(steps), extent[position] // parts).reshape((-1,) + (1,) * (len(extent) - position - 1))

    level = one(*shards[0])
    for cut in shards[1:]:
        level = level * one(*cut)
    return level


def profile(count, total, limit, lean):
    weights = [(1 << 20) // math.isqrt(grade ** lean) + 1 for grade in range(2, count + 1)]
    surplus, given = total - limit - (count - 1), [1] * (count - 1)
    while surplus > 0:
        free = [i for i in range(count - 1) if given[i] < limit]
        mass, budget = sum([weights[i] for i in free]), surplus
        for i in free:
            more = min(limit - given[i], max(1, budget * weights[i] // mass), surplus)
            given[i] = given[i] + more
            surplus = surplus - more
    return np.array([limit] + given)


def ragged(rng, amount, total, bound, slope):
    if amount == 2:
        one = jax.random.randint(rng, (), max(1, total - bound), min(bound, total - 1) + 1)
        return jnp.stack([one, total - one])
    sizes = jnp.asarray(profile(amount, total, bound, slope), jnp.int32)
    twos = (amount - 1) // 2
    source_of, taker = sizes[1:1 + 2 * twos:2], sizes[2:2 + 2 * twos:2]
    slack = jnp.minimum(source_of - 1, bound - taker)
    shifted = jax.random.randint(jax.random.fold_in(rng, 1), (twos,), 0, 1 << 20) % (slack + 1)
    sizes = sizes.at[1:1 + 2 * twos:2].set(source_of - shifted).at[2:2 + 2 * twos:2].set(taker + shifted)
    return sizes[jax.random.permutation(jax.random.fold_in(rng, 2), amount)]


def noise(key, shape, width, reach, shards=(), dtype=jnp.bfloat16):
    level = block_levels(key, shape, shards, -0.22, 0.18) if shards else 1.0
    values = jax.random.normal(key, shape, jnp.float32) * width * level
    return jnp.minimum(jnp.maximum(values, -reach), reach).astype(dtype)


def setup_inputs(seed: int = 0) -> dict:
    streams_of = jax.random.split(jax.random.key(seed), 19)
    return {
        "tokens": noise(streams_of[0], (ROWS, SEQ, D), 1.0, 6.0, ((0, 4), (1, 8))),
        "picture": jax.vmap(lambda own: jnp.searchsorted(jnp.cumsum(ragged(own, PICS, SEQ, MOST, 2)), jnp.arange(SEQ), side="right"))(jax.random.split(streams_of[1], ROWS)).reshape((ROWS, SEQ)).astype(jnp.int32),
        "ln1_gain": jnp.clip(1.0 + 0.1 * jax.random.normal(streams_of[2], (D,), jnp.float32), 0.5, 1.5),
        "ln1_bias": noise(streams_of[3], (D,), 0.2, 1.0, (), jnp.float32),
        "w_query": noise(streams_of[4], (D, D), D ** -0.5, 0.1875, ((0, 4), (1, 4))),
        "b_query": noise(streams_of[5], (D,), 0.2, 1.0, (), jnp.float32),
        "w_key": noise(streams_of[6], (D, D), D ** -0.5, 0.1875, ((0, 4), (1, 4))),
        "w_value": noise(streams_of[7], (D, D), D ** -0.5, 0.1875, ((0, 4), (1, 4))),
        "b_value": noise(streams_of[8], (D,), 0.2, 1.0, (), jnp.float32),
        "w_output": noise(streams_of[9], (D, D), (max(D // 512, 1)) ** -0.5, 4.0, ((0, 4), (1, 4))),
        "b_output": noise(streams_of[10], (D,), 0.2, 1.0, (), jnp.float32),
        "ln2_gain": jnp.clip(1.0 + 0.1 * jax.random.normal(streams_of[11], (D,), jnp.float32), 0.5, 1.5),
        "ln2_bias": noise(streams_of[12], (D,), 0.2, 1.0, (), jnp.float32),
        "w_first": noise(streams_of[13], (D, FF), D ** -0.5, 0.1875, ((0, 4), (1, 4))),
        "b_first": noise(streams_of[14], (FF,), 0.2, 1.0, (), jnp.float32),
        "w_second": noise(streams_of[15], (FF, D), FF ** -0.5, 0.09375, ((0, 4), (1, 4))),
        "b_second": noise(streams_of[16], (D,), 0.2, 1.0, (), jnp.float32),
        "cotangent": noise(streams_of[17], (ROWS, SEQ, D), 1.0, 6.0, ((0, 4), (1, 8))),
    }


@jax.custom_vjp
def low(v):
    return lax.optimization_barrier(v.astype(jnp.bfloat16)).astype(jnp.float32)

@jax.custom_vjp
def low_back(v):
    return v

def low_keep(v):
    return (low(v), None)

def low_pass(kept, grad):
    return (grad,)

def back_keep(v):
    return (v, None)

def back_low(kept, grad):
    return (low(grad),)
low.defvjp(low_keep, low_pass)
low_back.defvjp(back_keep, back_low)
EPSILON = 1e-06
HIGH = lax.Precision.HIGHEST

def matmul(left, right):
    return jnp.dot(left, right, precision=HIGH, preferred_element_type=jnp.float32)

def layer_norm(values, gain, bias):
    centred = values - lax.optimization_barrier(jnp.mean(values, axis=-1, keepdims=True))
    variance = lax.optimization_barrier(jnp.mean(centred * centred, axis=-1, keepdims=True))
    return centred * lax.rsqrt(variance + EPSILON) * gain + bias

def row_forward(params, row_input, row_ids):
    gain_one, bias_one, w_query, b_query, w_key, w_value, b_value, w_output, b_output, gain_two, bias_two, w_first, b_first, w_second, b_second = params
    normed = low(layer_norm(row_input, gain_one, bias_one))
    queries = low_back(low(matmul(normed, w_query) + b_query)).reshape(SEQ, HEADS, HD)
    keys = low_back(low(matmul(normed, w_key))).reshape(SEQ, HEADS, HD)
    values = low_back(low(matmul(normed, w_value) + b_value)).reshape(SEQ, HEADS, HD)
    scores = jnp.einsum('qhd,khd->hqk', queries, keys, precision=HIGH) * HD ** (-0.5)
    scores = low_back(scores)
    same = row_ids[:, None] == row_ids[None, :]
    scores = jnp.where(same[None, :, :], scores, -1e+30)
    probs = jax.nn.softmax(scores, axis=-1)
    attended = jnp.einsum('hqk,khd->qhd', low(probs), values, precision=HIGH).reshape(SEQ, D)
    attended = low_back(low(attended))
    attention = low_back(matmul(attended, w_output) + b_output)
    hidden = row_input + attention
    normed_two = low(layer_norm(hidden, gain_two, bias_two))
    before = low_back(matmul(normed_two, w_first) + b_first)
    active = low(jax.nn.gelu(before))
    return hidden + matmul(active, w_second) + b_second

def reference(tokens, picture, ln1_gain, ln1_bias, w_query, b_query, w_key, w_value, b_value, w_output, b_output, ln2_gain, ln2_bias, w_first, b_first, w_second, b_second, cotangent):
    params = (ln1_gain, ln1_bias, w_query.astype(jnp.float32), b_query, w_key.astype(jnp.float32), w_value.astype(jnp.float32), b_value, w_output.astype(jnp.float32), b_output, ln2_gain, ln2_bias, w_first.astype(jnp.float32), b_first, w_second.astype(jnp.float32), b_second)
    inputs = tokens.astype(jnp.float32)

    def whole(params_in, inputs_in):
        step = jax.checkpoint(lambda row_input, row_ids: row_forward(params_in, row_input, row_ids))

        def scan_step(carry, pair):
            return (carry, step(pair[0], pair[1]))
        _, results = lax.scan(scan_step, jnp.zeros((), jnp.float32), (inputs_in, picture))
        return results
    results, backward = jax.vjp(whole, params, inputs)
    grads, grad_inputs = backward(cotangent.astype(jnp.float32))
    return (results.astype(jnp.bfloat16), grad_inputs, grads[0], grads[1], grads[2], grads[3], grads[4], grads[5], grads[6], grads[7], grads[8], grads[9], grads[10], grads[11], grads[12], grads[13], grads[14])
```

```python
import functools

import jax
import jax.numpy as jnp
from jax import lax
from jax.experimental import pallas as pl
from jax.experimental.pallas import tpu as pltpu
from jax.sharding import PartitionSpec as P

HD = 72
EPSILON = 1e-06
LOG2E = 1.4426950408889634
NEG = -1e30
F32 = jnp.float32
BF16 = jnp.bfloat16


def dot(left, right, left_dim, right_dim):
    return lax.dot_general(
        left, right, (((left_dim,), (right_dim,)), ((), ())), preferred_element_type=F32
    )


def forward_kernel(nq, nk, bq, bk, count, index, q_ref, k_ref, v_ref, qid_ref, kid_ref, o_ref, lse_ref, kt):
    factor = HD ** (-0.5) * LOG2E
    kt[...] = k_ref[...].astype(F32).T.astype(BF16)
    for qb in range(nq):
        cols = pl.ds(qb * bq, bq)
        q = q_ref[:, cols]
        qid = qid_ref[:, cols]

        def body(n, carry):
            top, total, acc = carry
            off = pl.multiple_of(index[qb * nk + n] * bk, bk)
            s = dot(kt[pl.ds(off, bk), :], q, 1, 0) * factor
            s = jnp.where(kid_ref[pl.ds(off, bk), :] == qid, s, NEG)
            new = jnp.maximum(top, jnp.max(s, axis=0, keepdims=True))
            p = jnp.exp2(s - new)
            alpha = jnp.exp2(top - new)
            total = total * alpha + jnp.sum(p, axis=0, keepdims=True)
            acc = acc * alpha + dot(v_ref[:, pl.ds(off, bk)], p.astype(BF16), 1, 0)
            return new, total, acc

        top, total, acc = lax.fori_loop(
            0,
            count[qb],
            body,
            (jnp.full((1, bq), 4 * NEG, F32), jnp.zeros((1, bq), F32), jnp.zeros((HD, bq), F32)),
        )
        o_ref[:, cols] = (acc / total).astype(BF16)
        lse_ref[:, cols] = top + jnp.log2(total)


def backward_kernel(
    nq, nk, bq, bk, count, index, q_ref, k_ref, v_ref, do_ref, o_ref, lse_ref, qid_ref, kid_ref,
    dq_ref, dk_ref, dv_ref, kt, vt, dk_acc, dv_acc
):
    factor = HD ** (-0.5) * LOG2E
    kt[...] = k_ref[...].astype(F32).T.astype(BF16)
    vt[...] = v_ref[...].astype(F32).T.astype(BF16)
    dk_acc[...] = jnp.zeros_like(dk_acc)
    dv_acc[...] = jnp.zeros_like(dv_acc)
    for qb in range(nq):
        cols = pl.ds(qb * bq, bq)
        q = q_ref[:, cols]
        do = do_ref[:, cols]
        qid = qid_ref[:, cols]
        lse = lse_ref[:, cols]
        delta = jnp.sum(do.astype(F32) * o_ref[:, cols].astype(F32), axis=0, keepdims=True)

        def body(n, dq):
            off = pl.multiple_of(index[qb * nk + n] * bk, bk)
            rows = pl.ds(off, bk)
            s = dot(kt[rows, :], q, 1, 0) * factor
            p = jnp.exp2(jnp.where(kid_ref[rows, :] == qid, s, NEG) - lse)
            dp = dot(vt[rows, :], do, 1, 0)
            ds = (p * (dp - delta)).astype(BF16)
            dv_acc[:, rows] += dot(do, p.astype(BF16), 1, 1)
            dk_acc[:, rows] += dot(q, ds, 1, 1)
            return dq + dot(k_ref[:, rows], ds, 1, 0)

        dq = lax.fori_loop(0, count[qb], body, jnp.zeros((HD, bq), F32))
        dq_ref[:, cols] = (dq * HD ** (-0.5)).astype(BF16)
    dk_ref[...] = (dk_acc[...] * HD ** (-0.5)).astype(BF16)
    dv_ref[...] = dv_acc[...].astype(BF16)


def attention_forward(count, index, qt, kvt, qid, kid, bq, bk):
    width, tokens = qt.shape
    context = kvt.shape[1]
    heads = width // HD
    nq, nk = tokens // bq, context // bk
    q_spec = pl.BlockSpec((HD, tokens), lambda h, *_: (h, 0))
    k_spec = pl.BlockSpec((HD, context), lambda h, *_: (h, 0))
    v_spec = pl.BlockSpec((HD, context), lambda h, *_: (heads + h, 0))
    whole = lambda shape: pl.BlockSpec(shape, lambda h, *_: (0, 0))
    lse_spec = pl.BlockSpec((None, 1, tokens), lambda h, *_: (h, 0, 0))
    return pl.pallas_call(
        functools.partial(forward_kernel, nq, nk, bq, bk),
        out_shape=(
            jax.ShapeDtypeStruct((width, tokens), BF16),
            jax.ShapeDtypeStruct((heads, 1, tokens), F32),
        ),
        grid_spec=pltpu.PrefetchScalarGridSpec(
            num_scalar_prefetch=2,
            grid=(heads,),
            in_specs=[q_spec, k_spec, v_spec, whole((1, tokens)), whole((context, 1))],
            out_specs=(q_spec, lse_spec),
            scratch_shapes=[pltpu.VMEM((context, HD), BF16)],
        ),
        compiler_params=pltpu.CompilerParams(vmem_limit_bytes=48 << 20),
        cost_estimate=pl.CostEstimate(
            flops=tokens * context * width * 8, bytes_accessed=width * (tokens + context) * 4,
            transcendentals=tokens * context * heads // 2,
        ),
        name="attention_forward",
    )(count, index, qt, kvt, kvt, qid, kid)


def attention_backward(count, index, qt, kvt, dot_, ot, lse, qid, kid, bq, bk):
    width, tokens = qt.shape
    context = kvt.shape[1]
    heads = width // HD
    nq, nk = tokens // bq, context // bk
    q_spec = pl.BlockSpec((HD, tokens), lambda h, *_: (h, 0))
    k_spec = pl.BlockSpec((HD, context), lambda h, *_: (h, 0))
    v_spec = pl.BlockSpec((HD, context), lambda h, *_: (heads + h, 0))
    whole = lambda shape: pl.BlockSpec(shape, lambda h, *_: (0, 0))
    lse_spec = pl.BlockSpec((None, 1, tokens), lambda h, *_: (h, 0, 0))
    return pl.pallas_call(
        functools.partial(backward_kernel, nq, nk, bq, bk),
        out_shape=(
            jax.ShapeDtypeStruct((width, tokens), BF16),
            jax.ShapeDtypeStruct((width, context), BF16),
            jax.ShapeDtypeStruct((width, context), BF16),
        ),
        grid_spec=pltpu.PrefetchScalarGridSpec(
            num_scalar_prefetch=2,
            grid=(heads,),
            in_specs=[
                q_spec, k_spec, v_spec, q_spec, q_spec, lse_spec, whole((1, tokens)), whole((context, 1)),
            ],
            out_specs=(q_spec, k_spec, k_spec),
            scratch_shapes=[
                pltpu.VMEM((context, HD), BF16),
                pltpu.VMEM((context, HD), BF16),
                pltpu.VMEM((HD, context), F32),
                pltpu.VMEM((HD, context), F32),
            ],
        ),
        compiler_params=pltpu.CompilerParams(vmem_limit_bytes=48 << 20),
        cost_estimate=pl.CostEstimate(
            flops=tokens * context * width * 20, bytes_accessed=width * (tokens + context) * 8,
            transcendentals=tokens * context * heads // 2,
        ),
        name="attention_backward",
    )(count, index, qt, kvt, kvt, dot_, ot, lse, qid, kid)


def active_blocks(qid, kid, bq, bk):
    q = qid.reshape(-1, bq)
    k = kid.reshape(-1, bk)
    q_low, q_high = jnp.min(q, 1)[:, None], jnp.max(q, 1)[:, None]
    k_low, k_high = jnp.min(k, 1)[None, :], jnp.max(k, 1)[None, :]
    active = (q_low <= k_high) & (k_low <= q_high)
    slots = jnp.arange(k.shape[0], dtype=jnp.int32)
    before = (slots[:, None] < slots[None, :])[None]
    place = jnp.sum((active[:, :, None] & before).astype(jnp.int32), axis=1)
    hit = active[:, None, :] & (place[:, None, :] == slots[None, :, None])
    index = jnp.sum(jnp.where(hit, slots[None, None, :], 0), axis=2)
    return jnp.sum(active.astype(jnp.int32), axis=1), index.reshape(-1)


def norm_stats(values):
    centred = values - jnp.mean(values, axis=-1, keepdims=True)
    inverse = lax.rsqrt(jnp.mean(centred * centred, axis=-1, keepdims=True) + EPSILON)
    return centred * inverse, inverse


def norm_back(grad, scaled, inverse, gain):
    wide = grad * gain
    return inverse * (
        wide
        - jnp.mean(wide, axis=-1, keepdims=True)
        - scaled * jnp.mean(wide * scaled, axis=-1, keepdims=True)
    )


def gelu_pair(pre):
    c = 0.7978845608028654
    square = pre * pre
    t = jnp.tanh(c * pre * (1.0 + 0.044715 * square))
    value = 0.5 * pre * (1.0 + t)
    slope = 0.5 * (1.0 + t) + 0.5 * pre * (1.0 - t * t) * c * (1.0 + 3 * 0.044715 * square)
    return value, slope


def shards(
    sizes,
    tokens,
    picture,
    ln1_gain,
    ln1_bias,
    w_query,
    b_query,
    w_key,
    w_value,
    b_value,
    w_output,
    b_output,
    ln2_gain,
    ln2_bias,
    w_first,
    b_first,
    w_second,
    b_second,
    cotangent,
):
    tp, ctx = sizes["tp"], sizes["ctx"]
    rows, span, width = tokens.shape
    group = tp // rows
    place = lax.axis_index("tp")
    mine = place % rows
    row = place // group
    part = place % group

    def out_permutation(k):
        return [(s * rows + j, ((j + k) % rows) * group + s) for s in range(group) for j in range(rows)]

    def gather_row(blocks):
        got = []
        for k in range(rows):
            piece = lax.dynamic_index_in_dim(blocks, (mine + k) % rows, 0, keepdims=False)
            pairs = out_permutation(k)
            if any(a != b for a, b in pairs):
                piece = lax.ppermute(piece, "tp", pairs)
            got.append(piece)
        return got

    def scatter_row(values):
        out = jnp.zeros((rows, span) + values.shape[1:], values.dtype)
        for k in range(rows):
            piece = values[k * span : (k + 1) * span]
            pairs = [(b, a) for a, b in out_permutation(k)]
            if any(a != b for a, b in pairs):
                piece = lax.ppermute(piece, "tp", pairs)
            out = lax.dynamic_update_index_in_dim(out, piece, (mine + k) % rows, 0)
        return out

    def peers(step):
        s_step, c_step = step % group, step // group
        return s_step, c_step

    def fetch(value, step):
        s_step, c_step = peers(step)
        if s_step:
            pairs = [(r * group + (s + s_step) % group, r * group + s) for r in range(rows) for s in range(group)]
            value = lax.ppermute(value, "tp", pairs)
        if c_step:
            value = lax.ppermute(value, "ctx", [((c + c_step) % ctx, c) for c in range(ctx)])
        return value

    def give(value, step):
        s_step, c_step = peers(step)
        if s_step:
            pairs = [(r * group + s, r * group + (s + s_step) % group) for r in range(rows) for s in range(group)]
            value = lax.ppermute(value, "tp", pairs)
        if c_step:
            value = lax.ppermute(value, "ctx", [(c, (c + c_step) % ctx) for c in range(ctx)])
        return value

    steps = group * ctx

    heads_dev = w_query.shape[1]
    both = ("tp", "fsdp")
    qkvo = lax.all_gather(
        jnp.concatenate([w_query, w_key, w_value, w_output.T], axis=1), both, axis=0, tiled=True
    ).reshape(tp, width, 4, heads_dev)
    qkvo = qkvo.transpose(2, 0, 3, 1).reshape(4, tp * heads_dev, width)
    wq, wkv, wo = qkvo[0], qkvo[1:3].reshape(2 * tp * heads_dev, width), qkvo[3]
    units = w_first.shape[1]
    first = lax.all_gather(w_first, both, axis=0, tiled=True).reshape(tp, width, units)
    second = lax.all_gather(w_second.T, both, axis=0, tiled=True).reshape(tp, width, units)

    x16 = jnp.concatenate(gather_row(tokens), axis=0)
    count = rows * span
    ids = lax.dynamic_index_in_dim(picture, row, 0, keepdims=False).reshape(tp, span)
    order = part * rows + (row - jnp.arange(rows)) % rows
    ids = jnp.take(ids, order, axis=0).reshape(count)
    cot = jnp.concatenate(gather_row(cotangent), axis=0)
    x_all16 = jnp.concatenate([x16] + [fetch(x16, i) for i in range(1, steps)], axis=0)
    kid = jnp.concatenate([ids] + [fetch(ids, i) for i in range(1, steps)], axis=0)
    block = 256 if count % 256 == 0 else count
    blocks, index = active_blocks(ids, kid, block, block)
    qid, kid = ids[None, :], kid[:, None]

    x_all = x_all16.astype(F32)
    scaled_all, inverse_all = norm_stats(x_all)
    n1 = (scaled_all * ln1_gain + ln1_bias).astype(BF16)
    qt = (dot(wq, n1[:count], 1, 1) + b_query[:, None]).astype(BF16)
    kv_bias = jnp.concatenate([jnp.zeros_like(b_value), b_value])
    kvt = (dot(wkv, n1, 1, 1) + kv_bias[:, None]).astype(BF16)
    ot, lse = attention_forward(blocks, index, qt, kvt, qid, kid, block, block)
    h = x_all[:count] + (dot(ot, wo, 0, 0) + b_output)

    scaled2, inverse2 = norm_stats(h)
    n2 = (scaled2 * ln2_gain + ln2_bias).astype(BF16)
    y = h + b_second
    d_n2 = jnp.zeros_like(h)
    g_first, g_second, g_first_bias = [], [], []
    for t in range(tp):
        pre = dot(n2, first[t], 1, 0) + b_first[t * units : (t + 1) * units]
        value, slope = gelu_pair(pre)
        act = value.astype(BF16)
        y = y + dot(act, second[t], 1, 1)
        d_pre = (dot(cot, second[t], 1, 0) * slope).astype(BF16)
        d_n2 = d_n2 + dot(d_pre, first[t], 1, 1)
        g_second.append(dot(cot, act, 0, 0).astype(BF16))
        g_first.append(dot(n2, d_pre, 0, 0).astype(BF16))
        g_first_bias.append(jnp.sum(d_pre.astype(F32), axis=0))
    every = ("tp", "fsdp", "ctx")

    def scatter_grad(parts):
        return lax.psum_scatter(
            jnp.concatenate(parts, axis=0), every, scatter_dimension=0, tiled=True
        ).astype(F32)

    g_second = scatter_grad(g_second).T
    g_first = scatter_grad(g_first)
    output = scatter_row(y.astype(BF16))
    cot32 = cot.astype(F32)
    g_g2 = jnp.sum(d_n2 * scaled2, axis=0)
    g_c2 = jnp.sum(d_n2, axis=0)
    d_h = cot32 + norm_back(d_n2, scaled2, inverse2, ln2_gain)
    g_bs = jnp.sum(cot32, axis=0)

    d_att = d_h.astype(BF16)
    g_bo = jnp.sum(d_att.astype(F32), axis=0)
    d_ot = dot(wo, d_att, 1, 1).astype(BF16)
    dqt, dkt, dvt = attention_backward(blocks, index, qt, kvt, d_ot, ot, lse, qid, kid, block, block)
    d_all = dot(dkt, wkv[: tp * heads_dev], 0, 0) + dot(dvt, wkv[tp * heads_dev :], 0, 0)
    d_n1 = d_all[:count] + dot(dqt, wq, 0, 0)
    for i in range(1, steps):
        d_n1 = d_n1 + give(d_all[i * count : (i + 1) * count].astype(BF16), i).astype(F32)
    g_query = dot(n1[:count], dqt, 0, 1)
    g_key = dot(n1, dkt, 0, 1)
    g_value = dot(n1, dvt, 0, 1)
    g_out = dot(d_att, ot, 0, 1)
    g_bq = jnp.sum(dqt.astype(F32), axis=1)
    g_bv = jnp.sum(dvt.astype(F32), axis=1)

    def split(grad):
        return grad.astype(BF16).reshape(width, tp, heads_dev).transpose(1, 0, 2).reshape(tp * width, heads_dev)

    g_out = scatter_grad([split(g_out)]).T
    g_query, g_key, g_value = (scatter_grad([split(v)]) for v in (g_query, g_key, g_value))

    scaled1, inverse1 = scaled_all[:count], inverse_all[:count]
    g_g1 = jnp.sum(d_n1 * scaled1, axis=0)
    g_c1 = jnp.sum(d_n1, axis=0)
    grad_tokens = d_h + norm_back(d_n1, scaled1, inverse1, ln1_gain)
    grad_tokens = scatter_row(grad_tokens.astype(BF16)).astype(F32)

    small = lax.psum(
        (g_g1, g_c1, g_bq, g_bv, g_bo, g_g2, g_c2, jnp.concatenate(g_first_bias), g_bs),
        ("fsdp", "ctx", "tp"),
    )
    g_g1, g_c1, g_bq, g_bv, g_bo, g_g2, g_c2, g_bf, g_bs = small
    return (
        output, grad_tokens, g_g1, g_c1, g_query, g_bq, g_key, g_value, g_bv, g_out, g_bo,
        g_g2, g_c2, g_first, g_bf, g_second, g_bs,
    )


def solution(mesh):
    rows_spec = P("fsdp", ("ctx", "tp"), None)
    column, line = P("fsdp", "tp"), P("tp", "fsdp")
    column_out, line_out = P(("fsdp", "ctx"), "tp"), P("tp", ("fsdp", "ctx"))
    return jax.shard_map(
        functools.partial(shards, dict(mesh.shape)),
        mesh=mesh,
        in_specs=(
            rows_spec, P("fsdp", "ctx"), P(), P(), column, P(), column, column, P(), line, P(),
            P(), P(), column, P(), line, P(), rows_spec,
        ),
        out_specs=(
            rows_spec, rows_spec, P(), P(), column_out, P(), column_out, column_out, P(), line_out,
            P(), P(), P(), column_out, P(), line_out, P(),
        ),
        check_vma=False,
    )
```

```python
import functools

import jax
import jax.numpy as jnp
from jax import lax
from jax.experimental import pallas as pl
from jax.experimental.pallas import tpu as pltpu
from jax.sharding import PartitionSpec as P

HD = 72
PICS = 4
EPSILON = 1e-06
LOG2E = 1.4426950408889634
NEG = -1e30
F32 = jnp.float32
BF16 = jnp.bfloat16
MESH = pl.DeviceIdType.MESH


def dot(left, right, left_dim, right_dim):
    return lax.dot_general(
        left, right, (((left_dim,), (right_dim,)), ((), ())), preferred_element_type=F32
    )


def load_augmented(h, q_ref, k_ref, qm_ref, km_ref, kt, qa):
    rows = slice(h * HD, (h + 1) * HD)
    kt[h] = jnp.concatenate([k_ref[rows, :].astype(F32), km_ref[...]], axis=0).T.astype(BF16)
    qa[h] = jnp.concatenate([q_ref[rows, :].astype(F32), qm_ref[...]], axis=0).astype(BF16)


def forward_kernel(nq, nk, block, heads, count, index, q_ref, k_ref, v_ref, qm_ref, km_ref, o_ref, lse_ref, kt, qa):
    for h in range(heads):
        load_augmented(h, q_ref, k_ref, qm_ref, km_ref, kt, qa)
    for qb in range(nq):
        cols = pl.ds(qb * block, block)
        q = [qa[h, :, cols] for h in range(heads)]

        def body(n, carry):
            off = pl.multiple_of(index[qb * nk + n] * block, block)
            scores = [dot(kt[h, pl.ds(off, block), :], q[h], 1, 0) for h in range(heads)]
            out = []
            for h in range(heads):
                top, total, acc = carry[h]
                new = jnp.maximum(top, jnp.max(scores[h], axis=0, keepdims=True))
                p = jnp.exp2(scores[h] - new)
                alpha = jnp.exp2(top - new)
                total = total * alpha + jnp.sum(p, axis=0, keepdims=True)
                acc = acc * alpha + dot(v_ref[h * HD : (h + 1) * HD, pl.ds(off, block)], p.astype(BF16), 1, 0)
                out.append((new, total, acc))
            return tuple(out)

        start = (jnp.full((1, block), 4 * NEG, F32), jnp.zeros((1, block), F32), jnp.zeros((HD, block), F32))
        done = lax.fori_loop(0, count[qb], body, (start,) * heads)
        for h in range(heads):
            top, total, acc = done[h]
            o_ref[h * HD : (h + 1) * HD, cols] = (acc / total).astype(BF16)
            lse_ref[h, :, cols] = top + jnp.log2(total)


def backward_kernel(
    nq, nk, block, heads, count, index, q_ref, k_ref, v_ref, do_ref, o_ref, lse_ref, qm_ref, km_ref,
    dq_ref, dk_ref, dv_ref, kt, vt, qa, dk_acc, dv_acc
):
    for h in range(heads):
        load_augmented(h, q_ref, k_ref, qm_ref, km_ref, kt, qa)
        vt[h] = v_ref[h * HD : (h + 1) * HD, :].astype(F32).T.astype(BF16)
    dk_acc[...] = jnp.zeros_like(dk_acc)
    dv_acc[...] = jnp.zeros_like(dv_acc)
    for qb in range(nq):
        cols = pl.ds(qb * block, block)
        lines = [slice(h * HD, (h + 1) * HD) for h in range(heads)]
        q = [qa[h, :, cols] for h in range(heads)]
        do = [do_ref[lines[h], cols] for h in range(heads)]
        lse = [lse_ref[h, :, cols] for h in range(heads)]
        delta = [
            jnp.sum(do[h].astype(F32) * o_ref[lines[h], cols].astype(F32), axis=0, keepdims=True)
            for h in range(heads)
        ]

        def body(n, carry):
            rows = pl.ds(pl.multiple_of(index[qb * nk + n] * block, block), block)
            scores = [dot(kt[h, rows, :], q[h], 1, 0) for h in range(heads)]
            d_probs = [dot(vt[h, rows, :], do[h], 1, 0) for h in range(heads)]
            out = []
            for h in range(heads):
                p = jnp.exp2(scores[h] - lse[h])
                ds = (p * (d_probs[h] - delta[h])).astype(BF16)
                dv_acc[h, :, rows] += dot(do[h], p.astype(BF16), 1, 1)
                dk_acc[h, :, rows] += dot(q[h][:HD], ds, 1, 1)
                out.append(carry[h] + dot(k_ref[lines[h], rows], ds, 1, 0))
            return tuple(out)

        dq = lax.fori_loop(0, count[qb], body, (jnp.zeros((HD, block), F32),) * heads)
        for h in range(heads):
            dq_ref[lines[h], cols] = (dq[h] * HD ** (-0.5)).astype(BF16)
    for h in range(heads):
        dk_ref[h * HD : (h + 1) * HD, :] = (dk_acc[h] * (1.0 / LOG2E)).astype(BF16)
        dv_ref[h * HD : (h + 1) * HD, :] = dv_acc[h].astype(BF16)


def attention_specs(tokens, context, total, heads):
    q_spec = pl.BlockSpec((HD * heads, tokens), lambda h, *_: (h, 0))
    k_spec = pl.BlockSpec((HD * heads, context), lambda h, *_: (h, 0))
    v_spec = pl.BlockSpec((HD * heads, context), lambda h, *_: (total // heads + h, 0))
    lse_spec = pl.BlockSpec((heads, 1, tokens), lambda h, *_: (h, 0, 0))
    masks = [pl.BlockSpec((8, tokens), lambda h, *_: (0, 0)), pl.BlockSpec((8, context), lambda h, *_: (0, 0))]
    return q_spec, k_spec, v_spec, lse_spec, masks


def attention_forward(count, index, qt, kvt, qm, km, block, heads=8):
    width, tokens = qt.shape
    context, total = kvt.shape[1], width // HD
    q_spec, k_spec, v_spec, lse_spec, masks = attention_specs(tokens, context, total, heads)
    return pl.pallas_call(
        functools.partial(forward_kernel, tokens // block, context // block, block, heads),
        out_shape=(
            jax.ShapeDtypeStruct((width, tokens), BF16),
            jax.ShapeDtypeStruct((total, 1, tokens), F32),
        ),
        grid_spec=pltpu.PrefetchScalarGridSpec(
            num_scalar_prefetch=2,
            grid=(total // heads,),
            in_specs=[q_spec, k_spec, v_spec] + masks,
            out_specs=(q_spec, lse_spec),
            scratch_shapes=[pltpu.VMEM((heads, context, HD + 8), BF16), pltpu.VMEM((heads, HD + 8, tokens), BF16)],
        ),
        compiler_params=pltpu.CompilerParams(vmem_limit_bytes=56 << 20),
        cost_estimate=pl.CostEstimate(
            flops=tokens * context * width * 12, bytes_accessed=width * (tokens + context) * 4,
            transcendentals=tokens * context * total // 2,
        ),
        name="attention_forward",
    )(count, index, qt, kvt, kvt, qm, km)


def attention_backward(count, index, qt, kvt, d_ot, ot, lse, qm, km, block, heads=8):
    width, tokens = qt.shape
    context, total = kvt.shape[1], width // HD
    q_spec, k_spec, v_spec, lse_spec, masks = attention_specs(tokens, context, total, heads)
    return pl.pallas_call(
        functools.partial(backward_kernel, tokens // block, context // block, block, heads),
        out_shape=(
            jax.ShapeDtypeStruct((width, tokens), BF16),
            jax.ShapeDtypeStruct((width, context), BF16),
            jax.ShapeDtypeStruct((width, context), BF16),
        ),
        grid_spec=pltpu.PrefetchScalarGridSpec(
            num_scalar_prefetch=2,
            grid=(total // heads,),
            in_specs=[q_spec, k_spec, v_spec, q_spec, q_spec, lse_spec] + masks,
            out_specs=(q_spec, k_spec, k_spec),
            scratch_shapes=[
                pltpu.VMEM((heads, context, HD + 8), BF16),
                pltpu.VMEM((heads, context, HD), BF16),
                pltpu.VMEM((heads, HD + 8, tokens), BF16),
                pltpu.VMEM((heads, HD, context), F32),
                pltpu.VMEM((heads, HD, context), F32),
            ],
        ),
        compiler_params=pltpu.CompilerParams(vmem_limit_bytes=56 << 20),
        cost_estimate=pl.CostEstimate(
            flops=tokens * context * width * 20, bytes_accessed=width * (tokens + context) * 8,
            transcendentals=tokens * context * total // 2,
        ),
        name="attention_backward",
    )(count, index, qt, kvt, kvt, d_ot, ot, lse, qm, km)


def active_blocks(qid, kid, bq, bk):
    q = qid.reshape(-1, bq)
    k = kid.reshape(-1, bk)
    q_low, q_high = jnp.min(q, 1)[:, None], jnp.max(q, 1)[:, None]
    k_low, k_high = jnp.min(k, 1)[None, :], jnp.max(k, 1)[None, :]
    active = (q_low <= k_high) & (k_low <= q_high)
    slots = jnp.arange(k.shape[0], dtype=jnp.int32)
    before = (slots[:, None] < slots[None, :])[None]
    place = jnp.sum((active[:, :, None] & before).astype(jnp.int32), axis=1)
    hit = active[:, None, :] & (place[:, None, :] == slots[None, :, None])
    index = jnp.sum(jnp.where(hit, slots[None, None, :], 0), axis=2)
    return jnp.sum(active.astype(jnp.int32), axis=1), index.reshape(-1)


def norm_stats(values):
    centred = values - jnp.mean(values, axis=-1, keepdims=True)
    inverse = lax.rsqrt(jnp.mean(centred * centred, axis=-1, keepdims=True) + EPSILON)
    return centred * inverse, inverse


def norm_back(grad, scaled, inverse, gain):
    wide = grad * gain
    return inverse * (
        wide
        - jnp.mean(wide, axis=-1, keepdims=True)
        - scaled * jnp.mean(wide * scaled, axis=-1, keepdims=True)
    )


def gelu_pair(pre):
    c = 0.7978845608028654
    square = pre * pre
    t = jnp.tanh(c * pre * (1.0 + 0.044715 * square))
    value = 0.5 * pre * (1.0 + t)
    slope = 0.5 * (1.0 + t) + 0.5 * pre * (1.0 - t * t) * c * (1.0 + 3 * 0.044715 * square)
    return value, slope


def bits_of(size):
    assert size & (size - 1) == 0
    return size.bit_length() - 1


def exchange(value, axis, size, flip):
    return lax.ppermute(value, axis, [(i, i ^ flip) for i in range(size)])


def butterfly(value, sizes):
    for axis, size in sizes.items():
        for bit in range(bits_of(size)):
            value = value + exchange(value, axis, size, 1 << bit)
    return value


def halve(grad, sizes, ctx_first):
    fsdp, ctx = sizes["fsdp"], sizes["ctx"]
    nf, nc = bits_of(fsdp), bits_of(ctx)
    total = grad.reshape((2,) * (nf + nc) + (-1, grad.shape[-1])).astype(F32)
    f_stages = [("fsdp", fsdp, bit) for bit in range(nf)]
    c_stages = [("ctx", ctx, bit) for bit in range(nc)]
    stages = f_stages[:1] + (c_stages + f_stages[1:] if ctx_first else f_stages[1:] + c_stages)
    left = [("fsdp", bit) for bit in reversed(range(nf))] + [("ctx", bit) for bit in reversed(range(nc))]
    for axis, size, bit in stages:
        dim = left.index((axis, bit))
        mine = (lax.axis_index(axis) >> bit) & 1
        send = lax.dynamic_index_in_dim(total, 1 - mine, dim, keepdims=False).astype(BF16)
        keep = lax.dynamic_index_in_dim(total, mine, dim, keepdims=False)
        total = keep + exchange(send, axis, size, 1 << bit).astype(F32)
        left.pop(dim)
    return total


def scatter_units(parts, tp):
    place = lax.axis_index("tp")
    stack = jnp.stack([p.astype(BF16) for p in parts])
    total = lax.dynamic_index_in_dim(jnp.stack(parts), place, 0, keepdims=False)
    for k in range(1, tp):
        piece = lax.dynamic_index_in_dim(stack, place ^ k, 0, keepdims=False)
        total = total + exchange(piece, "tp", tp, k).astype(F32)
    return total


def closing_kernel(kinds, moved, tp, refs):
    jobs = len(kinds)
    grads, (vec, gt) = refs[:jobs], refs[jobs : jobs + 2]
    rest = list(refs[jobs + 2 :])

    def take(n):
        out = rest[:n]
        del rest[:n]
        return out

    units = sorted({slot for part, slot in kinds if part is not None})
    heads = sorted({slot for part, slot in kinds if part is None})
    out_units, out_heads = take(len(units)), take(len(heads))
    vec_out, gt_out = take(2)
    arrived = take(jobs)
    widths = [g.shape[-1] for g in grads]
    pools = {w: take(2) for w in sorted(set(widths))}
    slots = [widths[:j].count(widths[j]) % 2 for j in range(jobs)]
    own = [pools[widths[j]][0].at[slots[j]] for j in range(jobs)]
    come = [pools[widths[j]][1].at[slots[j]] for j in range(jobs)]
    keep, send2, recv2, send3, recv3 = (take(jobs) for _ in range(5))
    last_units, last_heads, piece_heads = take(len(units)), take(len(heads)), take(len(heads))
    (vec_in,) = take(1)
    s1, r1, s2, r2, s3, r3, l1, l2 = take(8)
    s4, r4, sv, rv, sg, rg, lg = take(7)

    f, c, z = lax.axis_index("fsdp"), lax.axis_index("ctx"), lax.axis_index("tp")
    x, core = f // 2, f % 2
    near, across = f + 1 - 2 * core, f + 2 - 4 * x
    other_c = 1 - c

    barrier = pltpu.get_barrier_semaphore()
    for where in ({"fsdp": near}, {"fsdp": across}, {"ctx": other_c}):
        pl.semaphore_signal(barrier, inc=1, device_id=where, device_id_type=MESH)
    for k in range(1, tp):
        pl.semaphore_signal(barrier, inc=1, device_id={"tp": lax.rem(z + k, tp)}, device_id_type=MESH)
    pl.semaphore_wait(barrier, 2 + tp)

    def remote(src, dst, send, recv, where):
        return pltpu.make_async_remote_copy(
            src_ref=src, dst_ref=dst, send_sem=send, recv_sem=recv, device_id=where, device_id_type=MESH
        )

    for k in range(tp if moved else 0):
        @pl.when(z != k)
        def _():
            remote(gt.at[k], gt_out.at[z], sg.at[k], rg.at[z], {"tp": k}).start()

        @pl.when(z == k)
        def _():
            pltpu.make_async_copy(gt.at[k], gt_out.at[z], lg).start()

    first = [remote(grads[j].at[:, 1 - core], arrived[j], s1.at[j], r1.at[j], {"fsdp": near}) for j in range(jobs)]
    mine = [pltpu.make_async_copy(grads[j].at[:, core], own[j], l1.at[j]) for j in range(jobs)]
    theirs = [pltpu.make_async_copy(arrived[j], come[j], l2.at[j]) for j in range(jobs)]
    for copy in first:
        copy.start()

    def turn(j):
        return j % 2 == 0

    second, third = [], []
    for j in range(jobs):
        where2 = {"fsdp": across} if turn(j) else {"ctx": other_c}
        where3 = {"ctx": other_c} if turn(j) else {"fsdp": across}
        second.append(remote(send2[j], recv2[j], s2.at[j], r2.at[j], where2))
        third.append(remote(send3[j], recv3[j], s3.at[j], r3.at[j], where3))

    def rows_loop(rows, body):
        tile = 48

        @pl.loop(0, rows // tile)
        def _(i):
            body(pl.ds(pl.multiple_of(i * tile, 16), tile))

    def stage1(j):
        mine[j].wait()
        theirs[j].wait()
        rows = send3[j].shape[0]
        for i in range(2):

            def body(r, i=i):
                if turn(j):
                    out_at, in_at = (1 - x, i), (x, i)
                else:
                    out_at, in_at = (i, 1 - c), (i, c)
                send2[j][i, r] = (own[j][out_at[0], out_at[1], r].astype(F32) + come[j][out_at[0], out_at[1], r].astype(F32)).astype(BF16)
                keep[j][i, r] = (own[j][in_at[0], in_at[1], r].astype(F32) + come[j][in_at[0], in_at[1], r].astype(F32)).astype(BF16)

            rows_loop(rows, body)
        second[j].start()

    def stage2(j):
        second[j].wait()
        at = c if turn(j) else x

        def body(r):
            send3[j][r] = (keep[j][1 - at, r].astype(F32) + recv2[j][1 - at, r].astype(F32)).astype(BF16)
            keep[j][at, r] = (keep[j][at, r].astype(F32) + recv2[j][at, r].astype(F32)).astype(BF16)

        rows_loop(send3[j].shape[0], body)
        third[j].start()

    def stage3(j):
        third[j].wait()
        at = c if turn(j) else x
        part, slot = kinds[j]
        if part is None:
            width = piece_heads[slot].shape[-1]

            def body(r):
                total = keep[j][at, r].astype(F32) + recv3[j][r].astype(F32)
                for t in range(tp):
                    piece_heads[slot][t, r] = total[:, t * width : (t + 1) * width].astype(BF16)

            rows_loop(send3[j].shape[0], body)
            for t in range(tp):
                @pl.when(z != t)
                def _():
                    remote(piece_heads[slot].at[t], last_heads[slot].at[z], s4.at[j, t], r4.at[len(units) + slot, z], {"tp": t}).start()
        else:

            def body(r):
                send3[j][r] = (keep[j][at, r].astype(F32) + recv3[j][r].astype(F32)).astype(BF16)

            rows_loop(send3[j].shape[0], body)

            @pl.when(z != part)
            def _():
                remote(send3[j], last_units[slot].at[z], s4.at[j, part], r4.at[slot, z], {"tp": part}).start()

    flips = [{"fsdp": near}, {"fsdp": across}, {"ctx": other_c}]
    bit = 1
    while bit < tp:
        flips.append({"tp": z + bit - 2 * bit * lax.rem(lax.div(z, bit), 2)})
        bit *= 2
    swaps = [remote(vec_out, vec_in.at[i], sv.at[i], rv.at[i], where) for i, where in enumerate(flips)]
    vec_out[...] = vec[...]
    swaps[0].start()

    def small(i):
        swaps[i].wait()
        vec_out[...] = vec_out[...] + vec_in[i]
        if i + 1 < len(swaps):
            swaps[i + 1].start()

    mine[0].start()
    first[0].wait()
    theirs[0].start()
    lag = 2
    for step in range(jobs + 2 * lag):
        if step + 1 < jobs:
            mine[step + 1].start()
            first[step + 1].wait()
            theirs[step + 1].start()
        if step < jobs:
            stage1(step)
        if 0 <= step - lag < jobs:
            stage2(step - lag)
        if 0 <= step - 2 * lag < jobs:
            stage3(step - 2 * lag)
        if step % 2 == 0 and step // 2 < len(swaps):
            small(step // 2)
    for i in range((jobs + 2 * lag + 1) // 2, len(swaps)):
        small(i)

    for j, (part, slot) in enumerate(kinds):
        for t in range(tp):
            if part is None:
                @pl.when(z != t)
                def _():
                    remote(piece_heads[slot].at[t], last_heads[slot].at[z], s4.at[j, t], r4.at[len(units) + slot, z], {"tp": t}).wait_send()
                    remote(piece_heads[slot].at[t], last_heads[slot].at[t], s4.at[j, t], r4.at[len(units) + slot, t], {"tp": t}).wait_recv()
            elif t == part:
                @pl.when(z != t)
                def _():
                    remote(send3[j], last_units[slot].at[z], s4.at[j, t], r4.at[slot, z], {"tp": t}).wait_send()

                @pl.when(z == t)
                def _():
                    for other in range(tp):
                        if other != t:
                            remote(send3[j], last_units[slot].at[other], s4.at[j, t], r4.at[slot, other], {"tp": t}).wait_recv()
                    last_units[slot][t] = send3[j][...]
    for slot in heads:
        last_heads[slot][z] = piece_heads[slot][z]
    for slots, last, out in ((units, last_units, out_units), (heads, last_heads, out_heads)):
        for slot in slots:

            def body(r, last=last, out=out, slot=slot):
                total = last[slot][0, r].astype(F32)
                for t in range(1, tp):
                    total = total + last[slot][t, r].astype(F32)
                out[slot][r] = total

            rows_loop(out[slot].shape[0], body)
    for k in range(tp if moved else 0):
        @pl.when(z != k)
        def _():
            remote(gt.at[k], gt_out.at[z], sg.at[k], rg.at[z], {"tp": k}).wait_send()
            remote(gt.at[k], gt_out.at[k], sg.at[k], rg.at[k], {"tp": k}).wait_recv()

        @pl.when(z == k)
        def _():
            pltpu.make_async_copy(gt.at[k], gt_out.at[z], lg).wait()


def closing(unit_grads, head_grads, vector, token_grads, tp):
    kinds, operands = [], []
    for t in range(tp if unit_grads else 0):
        for slot, parts in enumerate(unit_grads):
            kinds.append((t, slot))
            operands.append(parts[t])
    for slot, grad in enumerate(head_grads):
        kinds.append((None, slot))
        operands.append(grad)
    operands = [g.reshape((2, 2, 2, g.shape[0] // 8, g.shape[1])) for g in operands]
    rows = operands[0].shape[3]
    jobs = len(kinds)
    vmem, hbm = pl.BlockSpec(memory_space=pltpu.VMEM), pl.BlockSpec(memory_space=pl.ANY)
    heads_w = head_grads[0].shape[1] // tp
    units_w = unit_grads[0][0].shape[1] if unit_grads else 0
    out_shape = (
        [jax.ShapeDtypeStruct((rows, units_w), F32)] * len(unit_grads)
        + [jax.ShapeDtypeStruct((rows, heads_w), F32)] * len(head_grads)
        + [jax.ShapeDtypeStruct(vector.shape, F32), jax.ShapeDtypeStruct(token_grads.shape, token_grads.dtype)]
        + [jax.ShapeDtypeStruct((2, 2, rows, g.shape[-1]), BF16) for g in operands]
    )
    out_specs = [vmem] * (len(unit_grads) + len(head_grads) + 1) + [hbm] * (1 + jobs)
    widths = [g.shape[-1] for g in operands]
    scratch = [pltpu.VMEM((2, 2, 2, rows, w), BF16) for w in sorted(set(widths)) for _ in range(2)]
    scratch += [pltpu.VMEM((2, rows, w), BF16) for w in widths] * 3
    scratch += [pltpu.VMEM((rows, w), BF16) for w in widths] * 2
    scratch += [pltpu.VMEM((tp, rows, units_w), BF16)] * len(unit_grads)
    scratch += [pltpu.VMEM((tp, rows, heads_w), BF16)] * (2 * len(head_grads))
    swaps = 3 + bits_of(tp)
    scratch += [pltpu.VMEM((swaps,) + vector.shape, F32)]
    scratch += [pltpu.SemaphoreType.DMA((jobs,))] * 8
    scratch += [pltpu.SemaphoreType.DMA((jobs, tp)), pltpu.SemaphoreType.DMA((len(unit_grads) + len(head_grads), tp))]
    scratch += [pltpu.SemaphoreType.DMA((swaps,))] * 2 + [pltpu.SemaphoreType.DMA((tp,))] * 2 + [pltpu.SemaphoreType.DMA]
    outs = pl.pallas_call(
        lambda *refs: closing_kernel(kinds, True, tp, refs),
        out_shape=out_shape,
        in_specs=[hbm] * jobs + [vmem, hbm],
        out_specs=out_specs,
        scratch_shapes=scratch,
        compiler_params=pltpu.CompilerParams(collective_id=1, has_side_effects=True, vmem_limit_bytes=62 << 20),
        name="closing",
    )(*operands, vector, token_grads)
    n_u, n_h = len(unit_grads), len(head_grads)
    return outs[:n_u], outs[n_u : n_u + n_h], outs[n_u + n_h], outs[n_u + n_h + 1]


def shards(
    sizes,
    tokens,
    picture,
    ln1_gain,
    ln1_bias,
    w_query,
    b_query,
    w_key,
    w_value,
    b_value,
    w_output,
    b_output,
    ln2_gain,
    ln2_bias,
    w_first,
    b_first,
    w_second,
    b_second,
    cotangent,
):
    tp, ctx = sizes["tp"], sizes["ctx"]
    rows, span, width = tokens.shape
    group = tp // rows
    place = lax.axis_index("tp")
    mine = place % rows
    row = place // group
    part = place % group

    def out_permutation(k):
        return [(s * rows + j, ((j + k) % rows) * group + s) for s in range(group) for j in range(rows)]

    def gather_row(blocks):
        got = []
        for k in range(rows):
            piece = lax.dynamic_index_in_dim(blocks, (mine + k) % rows, 0, keepdims=False)
            pairs = out_permutation(k)
            if any(a != b for a, b in pairs):
                piece = lax.ppermute(piece, "tp", pairs)
            got.append(piece)
        return got

    def scatter_row(values):
        out = jnp.zeros((rows, span) + values.shape[1:], values.dtype)
        for k in range(rows):
            piece = values[k * span : (k + 1) * span]
            pairs = [(b, a) for a, b in out_permutation(k)]
            if any(a != b for a, b in pairs):
                piece = lax.ppermute(piece, "tp", pairs)
            out = lax.dynamic_update_index_in_dim(out, piece, (mine + k) % rows, 0)
        return out

    def peers(step):
        s_step, c_step = step % group, step // group
        return s_step, c_step

    def fetch(value, step):
        s_step, c_step = peers(step)
        if s_step:
            pairs = [(r * group + (s + s_step) % group, r * group + s) for r in range(rows) for s in range(group)]
            value = lax.ppermute(value, "tp", pairs)
        if c_step:
            value = lax.ppermute(value, "ctx", [((c + c_step) % ctx, c) for c in range(ctx)])
        return value

    def give(value, step):
        s_step, c_step = peers(step)
        if s_step:
            pairs = [(r * group + s, r * group + (s + s_step) % group) for r in range(rows) for s in range(group)]
            value = lax.ppermute(value, "tp", pairs)
        if c_step:
            value = lax.ppermute(value, "ctx", [(c, (c + c_step) % ctx) for c in range(ctx)])
        return value

    steps = group * ctx

    heads_dev = w_query.shape[1]
    both = ("tp", "fsdp")
    qkvo = lax.all_gather(
        jnp.concatenate([w_query, w_key, w_value, w_output.T], axis=1), both, axis=0, tiled=True
    ).reshape(tp, width, 4, heads_dev)
    qkvo = qkvo.transpose(2, 0, 3, 1).reshape(4, tp * heads_dev, width)
    wq, wkv, wo = qkvo[0], qkvo[1:3].reshape(2 * tp * heads_dev, width), qkvo[3]
    units = w_first.shape[1]
    first = lax.all_gather(w_first, both, axis=0, tiled=True).reshape(tp, width, units)
    second = lax.all_gather(w_second.T, both, axis=0, tiled=True).reshape(tp, width, units)

    x16 = jnp.concatenate(gather_row(tokens), axis=0)
    count = rows * span
    ids = lax.dynamic_index_in_dim(picture, row, 0, keepdims=False).reshape(tp, span)
    order = part * rows + (row - jnp.arange(rows)) % rows
    ids = jnp.take(ids, order, axis=0).reshape(count)
    cot = jnp.concatenate(gather_row(cotangent), axis=0)
    x_all16 = jnp.concatenate([x16] + [fetch(x16, i) for i in range(1, steps)], axis=0)
    kid = jnp.concatenate([ids] + [fetch(ids, i) for i in range(1, steps)], axis=0)
    block = 256 if count % 256 == 0 else count
    blocks, index = active_blocks(ids, kid, block, block)
    numbers = jnp.arange(8)[:, None]
    qm = jnp.where((numbers < PICS) & (ids[None, :] != numbers), NEG, 0.0).astype(F32)
    km = (kid[None, :] == numbers).astype(F32)

    x_all = x_all16.astype(F32)
    scaled_all, inverse_all = norm_stats(x_all)
    n1 = (scaled_all * ln1_gain + ln1_bias).astype(BF16)
    qt = ((dot(wq, n1[:count], 1, 1) + b_query[:, None]) * (HD ** (-0.5) * LOG2E)).astype(BF16)
    kv_bias = jnp.concatenate([jnp.zeros_like(b_value), b_value])
    kvt = (dot(wkv, n1, 1, 1) + kv_bias[:, None]).astype(BF16)
    ot, lse = attention_forward(blocks, index, qt, kvt, qm, km, block)
    h = x_all[:count] + (dot(ot, wo, 0, 0) + b_output)

    scaled2, inverse2 = norm_stats(h)
    n2 = (scaled2 * ln2_gain + ln2_bias).astype(BF16)
    y = h + b_second
    d_n2 = jnp.zeros_like(h)
    g_first, g_second, g_first_bias = [], [], []
    for t in range(tp):
        pre = dot(n2, first[t], 1, 0) + b_first[t * units : (t + 1) * units]
        value, slope = gelu_pair(pre)
        act = value.astype(BF16)
        y = y + dot(act, second[t], 1, 1)
        d_pre = (dot(cot, second[t], 1, 0) * slope).astype(BF16)
        d_n2 = d_n2 + dot(d_pre, first[t], 1, 1)
        g_second.append(dot(cot, act, 0, 0).astype(BF16))
        g_first.append(dot(n2, d_pre, 0, 0).astype(BF16))
        g_first_bias.append(jnp.sum(d_pre.astype(F32), axis=0))
    output = scatter_row(y.astype(BF16))
    cot32 = cot.astype(F32)
    g_g2 = jnp.sum(d_n2 * scaled2, axis=0)
    g_c2 = jnp.sum(d_n2, axis=0)
    d_h = cot32 + norm_back(d_n2, scaled2, inverse2, ln2_gain)
    g_bs = jnp.sum(cot32, axis=0)

    d_att = d_h.astype(BF16)
    g_bo = jnp.sum(d_att.astype(F32), axis=0)
    d_ot = dot(wo, d_att, 1, 1).astype(BF16)
    dqt, dkt, dvt = attention_backward(blocks, index, qt, kvt, d_ot, ot, lse, qm, km, block)
    d_all = dot(dkt, wkv[: tp * heads_dev], 0, 0) + dot(dvt, wkv[tp * heads_dev :], 0, 0)
    d_n1 = d_all[:count] + dot(dqt, wq, 0, 0)
    for i in range(1, steps):
        d_n1 = d_n1 + give(d_all[i * count : (i + 1) * count].astype(BF16), i).astype(F32)
    g_query = dot(n1[:count], dqt, 0, 1)
    g_key = dot(n1, dkt, 0, 1)
    g_value = dot(n1, dvt, 0, 1)
    g_out = dot(d_att, ot, 0, 1)
    g_bq = jnp.sum(dqt.astype(F32), axis=1)
    g_bv = jnp.sum(dvt.astype(F32), axis=1)

    scaled1, inverse1 = scaled_all[:count], inverse_all[:count]
    g_g1 = jnp.sum(d_n1 * scaled1, axis=0)
    g_c1 = jnp.sum(d_n1, axis=0)
    grad_tokens = (d_h + norm_back(d_n1, scaled1, inverse1, ln1_gain)).astype(BF16)
    small = [g_g1, g_c1, g_bq, g_bv, g_bo, g_g2, g_c2, jnp.concatenate(g_first_bias), g_bs]
    vector = jnp.concatenate(small)
    vector = jnp.pad(vector, (0, -vector.shape[0] % 1024)).reshape(-1, 128)
    head_grads = [g.astype(BF16) for g in (g_query, g_key, g_value, g_out)]
    if sizes["fsdp"] == 4 and ctx == 2 and group == 1 and bits_of(tp):
        natural = jnp.zeros((rows, span, width), BF16)
        for k in range(rows):
            piece = grad_tokens[k * span : (k + 1) * span]
            natural = lax.dynamic_update_index_in_dim(natural, piece, (place - k) % rows, 0)
        (g_first, g_second), heads_out, vector, grad_tokens = closing(
            [g_first, g_second], head_grads, vector, natural, tp
        )
        g_query, g_key, g_value, g_out = heads_out
    else:
        g_first, g_second = (
            scatter_units([halve(g, sizes, i % 2 == 0) for g in parts], tp)
            for i, parts in enumerate((g_first, g_second))
        )
        halved = [halve(g, sizes, i % 2 == 0) for i, g in enumerate(head_grads)]
        g_query, g_key, g_value, g_out = (
            scatter_units([g[:, t * heads_dev : (t + 1) * heads_dev] for t in range(tp)], tp) for g in halved
        )
        vector = butterfly(vector, sizes)
        grad_tokens = scatter_row(grad_tokens)
    grad_tokens = grad_tokens.astype(F32)
    g_out, g_second = g_out.T, g_second.T
    vector = vector.reshape(-1)
    ends = [sum(p.shape[0] for p in small[:i]) for i in range(len(small) + 1)]
    g_g1, g_c1, g_bq, g_bv, g_bo, g_g2, g_c2, g_bf, g_bs = (vector[i:j] for i, j in zip(ends, ends[1:]))
    return (
        output, grad_tokens, g_g1, g_c1, g_query, g_bq, g_key, g_value, g_bv, g_out, g_bo,
        g_g2, g_c2, g_first, g_bf, g_second, g_bs,
    )


def solution(mesh):
    rows_spec = P("fsdp", ("ctx", "tp"), None)
    column, line = P("fsdp", "tp"), P("tp", "fsdp")
    column_out, line_out = P(("fsdp", "ctx"), "tp"), P("tp", ("fsdp", "ctx"))
    return jax.shard_map(
        functools.partial(shards, dict(mesh.shape)),
        mesh=mesh,
        in_specs=(
            rows_spec, P("fsdp", "ctx"), P(), P(), column, P(), column, column, P(), line, P(),
            P(), P(), column, P(), line, P(), rows_spec,
        ),
        out_specs=(
            rows_spec, rows_spec, P(), P(), column_out, P(), column_out, column_out, P(), line_out,
            P(), P(), P(), column_out, P(), line_out, P(),
        ),
        check_vma=False,
    )
```

```python
import functools

import jax
import jax.numpy as jnp
from jax import lax
from jax.experimental import pallas as pl
from jax.experimental.pallas import tpu as pltpu
from jax.sharding import PartitionSpec as P

HD = 72
PICS = 4
EPSILON = 1e-06
LOG2E = 1.4426950408889634
NEG = -1e30
F32 = jnp.float32
BF16 = jnp.bfloat16
MESH = pl.DeviceIdType.MESH


def dot(left, right, left_dim, right_dim):
    return lax.dot_general(
        left, right, (((left_dim,), (right_dim,)), ((), ())), preferred_element_type=F32
    )


def load_augmented(h, q_ref, k_ref, qm_ref, km_ref, kt, qa):
    rows = slice(h * HD, (h + 1) * HD)
    kt[h] = jnp.concatenate([k_ref[rows, :].astype(F32), km_ref[...]], axis=0).T.astype(BF16)
    qa[h] = jnp.concatenate([q_ref[rows, :].astype(F32), qm_ref[...]], axis=0).astype(BF16)


def forward_kernel(nq, nk, block, heads, count, index, q_ref, k_ref, v_ref, qm_ref, km_ref, o_ref, lse_ref, kt, qa):
    for h in range(heads):
        load_augmented(h, q_ref, k_ref, qm_ref, km_ref, kt, qa)
    for qb in range(nq):
        cols = pl.ds(qb * block, block)
        q = [qa[h, :, cols] for h in range(heads)]

        def body(n, carry):
            off = pl.multiple_of(index[qb * nk + n] * block, block)
            scores = [dot(kt[h, pl.ds(off, block), :], q[h], 1, 0) for h in range(heads)]
            out = []
            for h in range(heads):
                top, total, acc = carry[h]
                new = jnp.maximum(top, jnp.max(scores[h], axis=0, keepdims=True))
                p = jnp.exp2(scores[h] - new)
                alpha = jnp.exp2(top - new)
                total = total * alpha + jnp.sum(p, axis=0, keepdims=True)
                acc = acc * alpha + dot(v_ref[h * HD : (h + 1) * HD, pl.ds(off, block)], p.astype(BF16), 1, 0)
                out.append((new, total, acc))
            return tuple(out)

        start = (jnp.full((1, block), 4 * NEG, F32), jnp.zeros((1, block), F32), jnp.zeros((HD, block), F32))
        done = lax.fori_loop(0, count[qb], body, (start,) * heads)
        for h in range(heads):
            top, total, acc = done[h]
            o_ref[h * HD : (h + 1) * HD, cols] = (acc / total).astype(BF16)
            lse_ref[h, :, cols] = top + jnp.log2(total)


def backward_kernel(
    nq, nk, block, heads, count, index, q_ref, k_ref, v_ref, do_ref, o_ref, lse_ref, qm_ref, km_ref,
    dq_ref, dk_ref, dv_ref, kt, vt, qa, dk_acc, dv_acc
):
    for h in range(heads):
        load_augmented(h, q_ref, k_ref, qm_ref, km_ref, kt, qa)
        vt[h] = v_ref[h * HD : (h + 1) * HD, :].astype(F32).T.astype(BF16)
    dk_acc[...] = jnp.zeros_like(dk_acc)
    dv_acc[...] = jnp.zeros_like(dv_acc)
    for qb in range(nq):
        cols = pl.ds(qb * block, block)
        lines = [slice(h * HD, (h + 1) * HD) for h in range(heads)]
        q = [qa[h, :, cols] for h in range(heads)]
        do = [do_ref[lines[h], cols] for h in range(heads)]
        lse = [lse_ref[h, :, cols] for h in range(heads)]
        delta = [
            jnp.sum(do[h].astype(F32) * o_ref[lines[h], cols].astype(F32), axis=0, keepdims=True)
            for h in range(heads)
        ]

        def body(n, carry):
            rows = pl.ds(pl.multiple_of(index[qb * nk + n] * block, block), block)
            scores = [dot(kt[h, rows, :], q[h], 1, 0) for h in range(heads)]
            d_probs = [dot(vt[h, rows, :], do[h], 1, 0) for h in range(heads)]
            out = []
            for h in range(heads):
                p = jnp.exp2(scores[h] - lse[h])
                ds = (p * (d_probs[h] - delta[h])).astype(BF16)
                dv_acc[h, :, rows] += dot(do[h], p.astype(BF16), 1, 1)
                dk_acc[h, :, rows] += dot(q[h][:HD], ds, 1, 1)
                out.append(carry[h] + dot(k_ref[lines[h], rows], ds, 1, 0))
            return tuple(out)

        dq = lax.fori_loop(0, count[qb], body, (jnp.zeros((HD, block), F32),) * heads)
        for h in range(heads):
            dq_ref[lines[h], cols] = (dq[h] * HD ** (-0.5)).astype(BF16)
    for h in range(heads):
        dk_ref[h * HD : (h + 1) * HD, :] = (dk_acc[h] * (1.0 / LOG2E)).astype(BF16)
        dv_ref[h * HD : (h + 1) * HD, :] = dv_acc[h].astype(BF16)


def attention_specs(tokens, context, total, heads):
    q_spec = pl.BlockSpec((HD * heads, tokens), lambda h, *_: (h, 0))
    k_spec = pl.BlockSpec((HD * heads, context), lambda h, *_: (h, 0))
    v_spec = pl.BlockSpec((HD * heads, context), lambda h, *_: (total // heads + h, 0))
    lse_spec = pl.BlockSpec((heads, 1, tokens), lambda h, *_: (h, 0, 0))
    masks = [pl.BlockSpec((8, tokens), lambda h, *_: (0, 0)), pl.BlockSpec((8, context), lambda h, *_: (0, 0))]
    return q_spec, k_spec, v_spec, lse_spec, masks


def attention_forward(count, index, qt, kvt, qm, km, block, heads=8):
    width, tokens = qt.shape
    context, total = kvt.shape[1], width // HD
    q_spec, k_spec, v_spec, lse_spec, masks = attention_specs(tokens, context, total, heads)
    return pl.pallas_call(
        functools.partial(forward_kernel, tokens // block, context // block, block, heads),
        out_shape=(
            jax.ShapeDtypeStruct((width, tokens), BF16),
            jax.ShapeDtypeStruct((total, 1, tokens), F32),
        ),
        grid_spec=pltpu.PrefetchScalarGridSpec(
            num_scalar_prefetch=2,
            grid=(total // heads,),
            in_specs=[q_spec, k_spec, v_spec] + masks,
            out_specs=(q_spec, lse_spec),
            scratch_shapes=[pltpu.VMEM((heads, context, HD + 8), BF16), pltpu.VMEM((heads, HD + 8, tokens), BF16)],
        ),
        compiler_params=pltpu.CompilerParams(vmem_limit_bytes=56 << 20),
        cost_estimate=pl.CostEstimate(
            flops=tokens * context * width * 12, bytes_accessed=width * (tokens + context) * 4,
            transcendentals=tokens * context * total // 2,
        ),
        name="attention_forward",
    )(count, index, qt, kvt, kvt, qm, km)


def attention_backward(count, index, qt, kvt, d_ot, ot, lse, qm, km, block, heads=8):
    width, tokens = qt.shape
    context, total = kvt.shape[1], width // HD
    q_spec, k_spec, v_spec, lse_spec, masks = attention_specs(tokens, context, total, heads)
    return pl.pallas_call(
        functools.partial(backward_kernel, tokens // block, context // block, block, heads),
        out_shape=(
            jax.ShapeDtypeStruct((width, tokens), BF16),
            jax.ShapeDtypeStruct((width, context), BF16),
            jax.ShapeDtypeStruct((width, context), BF16),
        ),
        grid_spec=pltpu.PrefetchScalarGridSpec(
            num_scalar_prefetch=2,
            grid=(total // heads,),
            in_specs=[q_spec, k_spec, v_spec, q_spec, q_spec, lse_spec] + masks,
            out_specs=(q_spec, k_spec, k_spec),
            scratch_shapes=[
                pltpu.VMEM((heads, context, HD + 8), BF16),
                pltpu.VMEM((heads, context, HD), BF16),
                pltpu.VMEM((heads, HD + 8, tokens), BF16),
                pltpu.VMEM((heads, HD, context), F32),
                pltpu.VMEM((heads, HD, context), F32),
            ],
        ),
        compiler_params=pltpu.CompilerParams(vmem_limit_bytes=56 << 20),
        cost_estimate=pl.CostEstimate(
            flops=tokens * context * width * 20, bytes_accessed=width * (tokens + context) * 8,
            transcendentals=tokens * context * total // 2,
        ),
        name="attention_backward",
    )(count, index, qt, kvt, kvt, d_ot, ot, lse, qm, km)


def active_blocks(qid, kid, bq, bk):
    q = qid.reshape(-1, bq)
    k = kid.reshape(-1, bk)
    q_low, q_high = jnp.min(q, 1)[:, None], jnp.max(q, 1)[:, None]
    k_low, k_high = jnp.min(k, 1)[None, :], jnp.max(k, 1)[None, :]
    active = (q_low <= k_high) & (k_low <= q_high)
    slots = jnp.arange(k.shape[0], dtype=jnp.int32)
    before = (slots[:, None] < slots[None, :])[None]
    place = jnp.sum((active[:, :, None] & before).astype(jnp.int32), axis=1)
    hit = active[:, None, :] & (place[:, None, :] == slots[None, :, None])
    index = jnp.sum(jnp.where(hit, slots[None, None, :], 0), axis=2)
    return jnp.sum(active.astype(jnp.int32), axis=1), index.reshape(-1)


def norm_stats(values):
    centred = values - jnp.mean(values, axis=-1, keepdims=True)
    inverse = lax.rsqrt(jnp.mean(centred * centred, axis=-1, keepdims=True) + EPSILON)
    return centred * inverse, inverse


def norm_back(grad, scaled, inverse, gain):
    wide = grad * gain
    return inverse * (
        wide
        - jnp.mean(wide, axis=-1, keepdims=True)
        - scaled * jnp.mean(wide * scaled, axis=-1, keepdims=True)
    )


def gelu_pair(pre):
    c = 0.7978845608028654
    square = pre * pre
    t = jnp.tanh(c * pre * (1.0 + 0.044715 * square))
    value = 0.5 * pre * (1.0 + t)
    slope = 0.5 * (1.0 + t) + 0.5 * pre * (1.0 - t * t) * c * (1.0 + 3 * 0.044715 * square)
    return value, slope


def bits_of(size):
    assert size & (size - 1) == 0
    return size.bit_length() - 1


def exchange(value, axis, size, flip):
    return lax.ppermute(value, axis, [(i, i ^ flip) for i in range(size)])


def butterfly(value, sizes):
    for axis, size in sizes.items():
        for bit in range(bits_of(size)):
            value = value + exchange(value, axis, size, 1 << bit)
    return value


def halve(grad, sizes, ctx_first):
    fsdp, ctx = sizes["fsdp"], sizes["ctx"]
    nf, nc = bits_of(fsdp), bits_of(ctx)
    total = grad.reshape((2,) * (nf + nc) + (-1, grad.shape[-1])).astype(F32)
    f_stages = [("fsdp", fsdp, bit) for bit in range(nf)]
    c_stages = [("ctx", ctx, bit) for bit in range(nc)]
    stages = f_stages[:1] + (c_stages + f_stages[1:] if ctx_first else f_stages[1:] + c_stages)
    left = [("fsdp", bit) for bit in reversed(range(nf))] + [("ctx", bit) for bit in reversed(range(nc))]
    for axis, size, bit in stages:
        dim = left.index((axis, bit))
        mine = (lax.axis_index(axis) >> bit) & 1
        send = lax.dynamic_index_in_dim(total, 1 - mine, dim, keepdims=False).astype(BF16)
        keep = lax.dynamic_index_in_dim(total, mine, dim, keepdims=False)
        total = keep + exchange(send, axis, size, 1 << bit).astype(F32)
        left.pop(dim)
    return total


def scatter_units(parts, tp):
    place = lax.axis_index("tp")
    stack = jnp.stack([p.astype(BF16) for p in parts])
    total = lax.dynamic_index_in_dim(jnp.stack(parts), place, 0, keepdims=False)
    for k in range(1, tp):
        piece = lax.dynamic_index_in_dim(stack, place ^ k, 0, keepdims=False)
        total = total + exchange(piece, "tp", tp, k).astype(F32)
    return total


def opening_kernel(
    tp, tokens, shard, ff_in, x_all, wt, ff, pieces,
    st, rt, sy, ry, sz, rz, sx, rx, sn, rn, own, fsz, frz, fsx, frx, fsy, fry, fsn, frn
):
    f, c, z = lax.axis_index("fsdp"), lax.axis_index("ctx"), lax.axis_index("tp")
    near, across = f + 1 - 2 * (f % 2), f + 2 - 4 * (f // 2)
    other_c = 1 - c

    barrier = pltpu.get_barrier_semaphore()
    for where in ({"fsdp": near}, {"fsdp": across}, {"ctx": other_c}):
        pl.semaphore_signal(barrier, inc=1, device_id=where, device_id_type=MESH)
    for k in range(1, tp):
        pl.semaphore_signal(barrier, inc=1, device_id={"tp": lax.rem(z + k, tp)}, device_id_type=MESH)
    start = pltpu.make_async_copy(shard, pieces.at[z, f], own.at[0])
    start.start()
    mine = [pltpu.make_async_copy(ff_in.at[m], ff.at[m, z, f], own.at[1 + m]) for m in range(2)]
    for copy in mine:
        copy.start()
    start.wait()
    pl.semaphore_wait(barrier, 2 + tp)

    def remote(src, dst, send, recv, where):
        return pltpu.make_async_remote_copy(
            src_ref=src, dst_ref=dst, send_sem=send, recv_sem=recv, device_id=where, device_id_type=MESH
        )

    def along(t, side):
        return remote(pieces.at[t, f], pieces.at[t, f], sz.at[t, side], rz.at[t], {"tp": z + 1 if side else z - 1})

    def cross(t):
        return remote(pieces.at[t, f], pieces.at[t, f], sx.at[t], rx.at[t], {"fsdp": across})

    def beside(t, i):
        source = across if i else f
        return remote(pieces.at[t, source], pieces.at[t, source], sn.at[t, i], rn.at[t, i], {"fsdp": near})

    def token(k, row):
        return remote(tokens.at[k], x_all.at[0, row], st.at[k], rt.at[row], {"tp": k})

    def half(t):
        return remote(x_all.at[0, t], x_all.at[1, t], sy.at[t], ry.at[t], {"ctx": other_c})

    def ff_along(t, side):
        part = ff.at[c, t, f]
        return remote(part, part, fsz.at[t, side], frz.at[t], {"tp": z + 1 if side else z - 1})

    def ff_cross(m, t):
        part = ff.at[m, t, f]
        return remote(part, part, fsx.at[m, t], frx.at[m, t], {"fsdp": across})

    def ff_half(t, i):
        part = ff.at[c, t, across if i else f]
        return remote(part, part, fsy.at[t, i], fry.at[t, i], {"ctx": other_c})

    def ff_beside(m, t, i):
        part = ff.at[m, t, across if i else f]
        return remote(part, part, fsn.at[m, t, i], frn.at[m, t, i], {"fsdp": near})

    def passes(t, right, left):
        @pl.when((t <= z) & (z < tp - 1))
        def _():
            right(t)

        @pl.when((t >= z) & (z > 0))
        def _():
            left(t)

    def onward(t):
        passes(t, lambda t: along(t, 1).start(), lambda t: along(t, 0).start())
        cross(t).start()
        beside(t, 0).start()

    def ff_pass(t):
        passes(t, lambda t: ff_along(t, 1).start(), lambda t: ff_along(t, 0).start())

    def arrivals(d, wait, then):
        for t, there in ((z - d, z >= d), (z + d, z + d < tp)):
            @pl.when(there)
            def _():
                wait(t)
                then(t)

    onward(z)
    local = pltpu.make_async_copy(tokens.at[z], x_all.at[0, z], own.at[0])
    local.start()
    for k in range(1, tp):
        token(z ^ k, z).start()
    for m in range(2):
        mine[m].wait()
        ff_cross(m, z).start()
        ff_beside(m, z, 0).start()
    local.wait()
    half(z).start()
    for d in range(1, tp):
        arrivals(d, lambda t: along(t, 0).wait_recv(), onward)
        block = z ^ d
        token(block, block).wait_recv()
        half(block).start()
        cross(z ^ (d - 1)).wait_recv()
        beside(z ^ (d - 1), 1).start()
        if d == 1:
            ff_pass(z)
    cross(z ^ (tp - 1)).wait_recv()
    beside(z ^ (tp - 1), 1).start()

    depth = shard.shape[0]
    columns = shard.shape[1] // 4

    def turn(t):
        for i in range(2):
            beside(t, i).wait_recv()
        for g in range(4):
            for w in range(4):
                piece = pieces[t, g, :, w * columns : (w + 1) * columns].astype(F32).T.astype(BF16)
                wt[w, pl.ds(pl.multiple_of(t * columns, 32), columns), g * depth : (g + 1) * depth] = piece

    def ff_onward(t):
        ff_pass(t)
        ff_cross(c, t).start()
        ff_half(t, 0).start()
        ff_beside(c, t, 0).start()

    def ff_second(t):
        ff_cross(c, t).wait_recv()
        ff_half(t, 1).start()
        ff_beside(c, t, 1).start()

    for d in range(1, tp):
        arrivals(d, lambda t: ff_along(t, 0).wait_recv(), ff_onward)
        if d == 1:
            for m in range(2):
                ff_cross(m, z).wait_recv()
                ff_beside(m, z, 1).start()
        else:
            arrivals(d - 1, lambda t: None, ff_second)
        turn(z ^ (d - 1))
    turn(z ^ (tp - 1))
    arrivals(tp - 1, lambda t: None, ff_second)
    for d in range(1, tp):

        def handed(t):
            for i in range(2):
                ff_half(t, i).wait_recv()
                ff_beside(1 - c, t, i).start()

        arrivals(d, lambda t: None, handed)

    for k in range(tp):
        t = z ^ k
        passes(t, lambda t: along(t, 1).wait_send(), lambda t: along(t, 0).wait_send())
        passes(t, lambda t: ff_along(t, 1).wait_send(), lambda t: ff_along(t, 0).wait_send())
        cross(t).wait_send()
        beside(t, 0).wait_send()
        beside(t, 1).wait_send()
        if k:
            token(t, z).wait_send()
        half(t).wait()
        for m in range(2):
            if k == 0:
                ff_cross(m, t).wait_send()
            for i in range(2):
                ff_beside(m, t, i).wait()
        if k:
            ff_cross(c, t).wait_send()
            for i in range(2):
                ff_half(t, i).wait_send()


def opening(tokens, shard, ff_in, tp):
    rows, span, width = tokens.shape
    vmem, hbm = pl.BlockSpec(memory_space=pltpu.VMEM), pl.BlockSpec(memory_space=pl.ANY)
    depth, columns = shard.shape[0], shard.shape[1] // 4
    dma = pltpu.SemaphoreType.DMA
    return pl.pallas_call(
        functools.partial(opening_kernel, tp),
        out_shape=(
            jax.ShapeDtypeStruct((2, rows, span, width), BF16),
            jax.ShapeDtypeStruct((4, tp * columns, 4 * depth), BF16),
            jax.ShapeDtypeStruct((2, tp, 4) + ff_in.shape[1:], BF16),
        ),
        in_specs=[hbm, hbm, hbm],
        out_specs=(hbm, vmem, hbm),
        scratch_shapes=[pltpu.VMEM((tp, 4, depth, 4 * columns), BF16)]
        + [dma((tp,))] * 4
        + [dma((tp, 2)), dma((tp,)), dma((tp,)), dma((tp,)), dma((tp, 2)), dma((tp, 2)), dma((3,))]
        + [dma((tp, 2)), dma((tp,)), dma((2, tp)), dma((2, tp)), dma((tp, 2)), dma((tp, 2))]
        + [dma((2, tp, 2)), dma((2, tp, 2))],
        compiler_params=pltpu.CompilerParams(collective_id=2, has_side_effects=True, vmem_limit_bytes=48 << 20),
        name="opening",
    )(tokens, shard, ff_in)


def feed_kernel(
    tp, n2, cot, bias, ff, y, dn2, g_first, g_second, g_bias,
    n2t, cott, weights, act, d_pre, near_part, recv1, recv2, recv3, recvz,
    lw, s1, r1, s2, r2, s3, r3, s4, r4
):
    f, c, z = lax.axis_index("fsdp"), lax.axis_index("ctx"), lax.axis_index("tp")
    x, core = f // 2, f % 2
    near, across, other_c = f + 1 - 2 * core, f + 2 - 4 * x, 1 - c
    tokens, width = n2.shape
    depth = width // 4
    order = list(range(tp - 1, -1, -1))

    def load(i):
        return [pltpu.make_async_copy(ff.at[m, z ^ order[i]], weights.at[m], lw.at[m]) for m in range(2)]

    for copy in load(0):
        copy.start()

    barrier = pltpu.get_barrier_semaphore()
    for where in ({"fsdp": near}, {"fsdp": across}, {"ctx": other_c}):
        pl.semaphore_signal(barrier, inc=1, device_id=where, device_id_type=MESH)
    for k in range(1, tp):
        pl.semaphore_signal(barrier, inc=1, device_id={"tp": z ^ k}, device_id_type=MESH)

    @pl.loop(0, width // 128)
    def _(i):
        part = pl.ds(pl.multiple_of(i * 128, 128), 128)
        n2t[part, :] = n2[:, part].astype(F32).T.astype(BF16)
        cott[part, :] = cot[:, part].astype(F32).T.astype(BF16)

    y[...] = jnp.zeros_like(y)
    dn2[...] = jnp.zeros_like(dn2)
    pl.semaphore_wait(barrier, 2 + tp)

    def remote(src, dst, send, recv, where):
        return pltpu.make_async_remote_copy(
            src_ref=src, dst_ref=dst, send_sem=send, recv_sem=recv, device_id=where, device_id_type=MESH
        )

    def first(j, m):
        return remote(near_part.at[m], recv1.at[j], s1.at[j], r1.at[j], {"fsdp": near})

    def second(j, m):
        if m == 0:
            return remote(recv1.at[j, 1 - x], recv2.at[j], s2.at[j], r2.at[j], {"fsdp": across})
        return remote(recv1.at[j, :, 1 - c], recv2.at[j], s2.at[j], r2.at[j], {"ctx": other_c})

    def third(j, m):
        if m == 0:
            return remote(recv2.at[j, 1 - c], recv3.at[j], s3.at[j], r3.at[j], {"ctx": other_c})
        return remote(recv2.at[j, 1 - x], recv3.at[j], s3.at[j], r3.at[j], {"fsdp": across})

    def last(j, m, k):
        return remote(recv3.at[j], recvz.at[m, k - 1], s4.at[m, k - 1], r4.at[m, k - 1], {"tp": z ^ k})

    half = depth // 2
    tile = 48

    def stage2(i):
        for m in range(2):
            j = 2 * i + m
            second(j, m).wait()

            @pl.loop(0, half // tile)
            def _(n):
                r = pl.ds(pl.multiple_of(n * tile, 16), tile)
                for a in range(2):
                    kept = recv1[j, x, a, r] if m == 0 else recv1[j, a, c, r]
                    recv2[j, a, r] = (kept.astype(F32) + recv2[j, a, r].astype(F32)).astype(BF16)

            third(j, m).start()

    def stage3(i):
        for m in range(2):
            j = 2 * i + m
            third(j, m).wait()

            @pl.loop(0, half // tile)
            def _(n):
                r = pl.ds(pl.multiple_of(n * tile, 16), tile)
                recv3[j, r] = (recv2[j, c if m == 0 else x, r].astype(F32) + recv3[j, r].astype(F32)).astype(BF16)

            if order[i]:
                last(j, m, order[i]).start()

    rows_tile = 256
    for i in range(tp):
        for copy in load(i):
            copy.wait()
        t = z ^ order[i]
        g_bias[t] = jnp.zeros_like(g_bias[t])

        @pl.loop(0, tokens // rows_tile)
        def _(n):
            r = pl.ds(pl.multiple_of(n * rows_tile, rows_tile), rows_tile)
            value, slope = gelu_pair(dot(n2[r, :], weights[0], 1, 0) + bias[t])
            act[r, :] = value.astype(BF16)
            back = (dot(cot[r, :], weights[1], 1, 0) * slope).astype(BF16)
            d_pre[r, :] = back
            g_bias[t] += jnp.sum(back.astype(F32), axis=0, keepdims=True)
            y[r, :] += dot(act[r, :], weights[1], 1, 1)
            dn2[r, :] += dot(back, weights[0], 1, 1)

        if i + 1 < tp:
            for copy in load(i + 1):
                copy.start()
        if i:
            stage2(i - 1)
        sides = ((n2t, d_pre), (cott, act))
        for m, (left, right) in enumerate(sides):
            j = 2 * i + m
            if i:
                first(j - 2, m).wait_send()

            @pl.loop(0, 2)
            def _(a):
                rows = pl.ds(pl.multiple_of((2 * a + 1 - core) * depth, 32), depth)
                grad = dot(left[rows, :], right[...], 1, 0).astype(BF16)
                for b in range(2):
                    near_part[m, a, b] = grad[b * half : (b + 1) * half]

            first(j, m).start()
        if i:
            stage3(i - 1)
        for m, (left, right) in enumerate(sides):
            j = 2 * i + m
            first(j, m).wait_recv()

            @pl.loop(0, 2)
            def _(a):
                rows = pl.ds(pl.multiple_of((2 * a + core) * depth, 32), depth)
                grad = dot(left[rows, :], right[...], 1, 0)
                for b in range(2):
                    recv1[j, a, b] = (grad[b * half : (b + 1) * half] + recv1[j, a, b].astype(F32)).astype(BF16)

            second(j, m).start()
    stage2(tp - 1)
    stage3(tp - 1)
    for m, out in enumerate((g_first, g_second)):
        first(2 * (tp - 1) + m, m).wait_send()
        for k in range(1, tp):
            last(2 * (tp - 1 - k) + m, m, k).wait()

        @pl.loop(0, half // tile)
        def _(n):
            r = pl.ds(pl.multiple_of(n * tile, 16), tile)
            total = recv3[2 * (tp - 1) + m, r].astype(F32)
            for k in range(1, tp):
                total = total + recvz[m, k - 1, r].astype(F32)
            out[r] = total


def feed(n2, cot, bias, ff, tp):
    tokens, width = n2.shape
    units, half = ff.shape[-1], width // 8
    vmem, hbm = pl.BlockSpec(memory_space=pltpu.VMEM), pl.BlockSpec(memory_space=pl.ANY)
    dma = pltpu.SemaphoreType.DMA
    return pl.pallas_call(
        functools.partial(feed_kernel, tp),
        out_shape=(
            jax.ShapeDtypeStruct((tokens, width), F32),
            jax.ShapeDtypeStruct((tokens, width), F32),
            jax.ShapeDtypeStruct((half, units), F32),
            jax.ShapeDtypeStruct((half, units), F32),
            jax.ShapeDtypeStruct((tp, 1, units), F32),
        ),
        in_specs=[vmem, vmem, vmem, hbm],
        out_specs=(vmem,) * 5,
        scratch_shapes=[
            pltpu.VMEM((width, tokens), BF16),
            pltpu.VMEM((width, tokens), BF16),
            pltpu.VMEM((2, width, units), BF16),
            pltpu.VMEM((tokens, units), BF16),
            pltpu.VMEM((tokens, units), BF16),
            pltpu.VMEM((2, 2, 2, half, units), BF16),
            pltpu.VMEM((2 * tp, 2, 2, half, units), BF16),
            pltpu.VMEM((2 * tp, 2, half, units), BF16),
            pltpu.VMEM((2 * tp, half, units), BF16),
            pltpu.VMEM((2, tp - 1, half, units), BF16),
            dma((2,)),
        ]
        + [dma((2 * tp,))] * 6
        + [dma((2, tp - 1))] * 2,
        compiler_params=pltpu.CompilerParams(collective_id=3, has_side_effects=True, vmem_limit_bytes=63 << 20),
        cost_estimate=pl.CostEstimate(
            flops=12 * tokens * width * tp * units, bytes_accessed=4 * width * tp * units + 16 * tokens * width,
            transcendentals=tokens * tp * units,
        ),
        name="feed",
    )(n2, cot, bias, ff)


def closing_kernel(kinds, moved, tp, refs):
    jobs = len(kinds)
    grads, (vec, gt) = refs[:jobs], refs[jobs : jobs + 2]
    rest = list(refs[jobs + 2 :])

    def take(n):
        out = rest[:n]
        del rest[:n]
        return out

    units = sorted({slot for part, slot in kinds if part is not None})
    heads = sorted({slot for part, slot in kinds if part is None})
    out_units, out_heads = take(len(units)), take(len(heads))
    vec_out, gt_out = take(2)
    arrived = take(jobs)
    widths = [g.shape[-1] for g in grads]
    pools = {w: take(2) for w in sorted(set(widths))}
    slots = [widths[:j].count(widths[j]) % 2 for j in range(jobs)]
    own = [pools[widths[j]][0].at[slots[j]] for j in range(jobs)]
    come = [pools[widths[j]][1].at[slots[j]] for j in range(jobs)]
    keep, send2, recv2, send3, recv3 = (take(jobs) for _ in range(5))
    last_units, last_heads, piece_heads = take(len(units)), take(len(heads)), take(len(heads))
    (vec_in,) = take(1)
    s1, r1, s2, r2, s3, r3, l1, l2 = take(8)
    s4, r4, sv, rv, sg, rg, lg = take(7)

    f, c, z = lax.axis_index("fsdp"), lax.axis_index("ctx"), lax.axis_index("tp")
    x, core = f // 2, f % 2
    near, across = f + 1 - 2 * core, f + 2 - 4 * x
    other_c = 1 - c

    barrier = pltpu.get_barrier_semaphore()
    for where in ({"fsdp": near}, {"fsdp": across}, {"ctx": other_c}):
        pl.semaphore_signal(barrier, inc=1, device_id=where, device_id_type=MESH)
    for k in range(1, tp):
        pl.semaphore_signal(barrier, inc=1, device_id={"tp": lax.rem(z + k, tp)}, device_id_type=MESH)
    pl.semaphore_wait(barrier, 2 + tp)

    def remote(src, dst, send, recv, where):
        return pltpu.make_async_remote_copy(
            src_ref=src, dst_ref=dst, send_sem=send, recv_sem=recv, device_id=where, device_id_type=MESH
        )

    for k in range(tp if moved else 0):
        @pl.when(z != k)
        def _():
            remote(gt.at[k], gt_out.at[z], sg.at[k], rg.at[z], {"tp": k}).start()

        @pl.when(z == k)
        def _():
            pltpu.make_async_copy(gt.at[k], gt_out.at[z], lg).start()

    first = [remote(grads[j].at[:, 1 - core], arrived[j], s1.at[j], r1.at[j], {"fsdp": near}) for j in range(jobs)]
    mine = [pltpu.make_async_copy(grads[j].at[:, core], own[j], l1.at[j]) for j in range(jobs)]
    theirs = [pltpu.make_async_copy(arrived[j], come[j], l2.at[j]) for j in range(jobs)]
    for copy in first:
        copy.start()

    def turn(j):
        return j % 2 == 0

    second, third = [], []
    for j in range(jobs):
        where2 = {"fsdp": across} if turn(j) else {"ctx": other_c}
        where3 = {"ctx": other_c} if turn(j) else {"fsdp": across}
        second.append(remote(send2[j], recv2[j], s2.at[j], r2.at[j], where2))
        third.append(remote(send3[j], recv3[j], s3.at[j], r3.at[j], where3))

    def rows_loop(rows, body):
        tile = 48

        @pl.loop(0, rows // tile)
        def _(i):
            body(pl.ds(pl.multiple_of(i * tile, 16), tile))

    def stage1(j):
        mine[j].wait()
        theirs[j].wait()
        rows = send3[j].shape[0]
        for i in range(2):

            def body(r, i=i):
                if turn(j):
                    out_at, in_at = (1 - x, i), (x, i)
                else:
                    out_at, in_at = (i, 1 - c), (i, c)
                send2[j][i, r] = (own[j][out_at[0], out_at[1], r].astype(F32) + come[j][out_at[0], out_at[1], r].astype(F32)).astype(BF16)
                keep[j][i, r] = (own[j][in_at[0], in_at[1], r].astype(F32) + come[j][in_at[0], in_at[1], r].astype(F32)).astype(BF16)

            rows_loop(rows, body)
        second[j].start()

    def stage2(j):
        second[j].wait()
        at = c if turn(j) else x

        def body(r):
            send3[j][r] = (keep[j][1 - at, r].astype(F32) + recv2[j][1 - at, r].astype(F32)).astype(BF16)
            keep[j][at, r] = (keep[j][at, r].astype(F32) + recv2[j][at, r].astype(F32)).astype(BF16)

        rows_loop(send3[j].shape[0], body)
        third[j].start()

    def stage3(j):
        third[j].wait()
        at = c if turn(j) else x
        part, slot = kinds[j]
        if part is None:
            width = piece_heads[slot].shape[-1]

            def body(r):
                total = keep[j][at, r].astype(F32) + recv3[j][r].astype(F32)
                for t in range(tp):
                    piece_heads[slot][t, r] = total[:, t * width : (t + 1) * width].astype(BF16)

            rows_loop(send3[j].shape[0], body)
            for t in range(tp):
                @pl.when(z != t)
                def _():
                    remote(piece_heads[slot].at[t], last_heads[slot].at[z], s4.at[j, t], r4.at[len(units) + slot, z], {"tp": t}).start()
        else:

            def body(r):
                send3[j][r] = (keep[j][at, r].astype(F32) + recv3[j][r].astype(F32)).astype(BF16)

            rows_loop(send3[j].shape[0], body)

            @pl.when(z != part)
            def _():
                remote(send3[j], last_units[slot].at[z], s4.at[j, part], r4.at[slot, z], {"tp": part}).start()

    flips = [{"fsdp": near}, {"fsdp": across}, {"ctx": other_c}]
    bit = 1
    while bit < tp:
        flips.append({"tp": z + bit - 2 * bit * lax.rem(lax.div(z, bit), 2)})
        bit *= 2
    swaps = [remote(vec_out, vec_in.at[i], sv.at[i], rv.at[i], where) for i, where in enumerate(flips)]
    vec_out[...] = vec[...]
    swaps[0].start()

    def small(i):
        swaps[i].wait()
        vec_out[...] = vec_out[...] + vec_in[i]
        if i + 1 < len(swaps):
            swaps[i + 1].start()

    mine[0].start()
    first[0].wait()
    theirs[0].start()
    lag = 2
    for step in range(jobs + 2 * lag):
        if step + 1 < jobs:
            mine[step + 1].start()
            first[step + 1].wait()
            theirs[step + 1].start()
        if step < jobs:
            stage1(step)
        if 0 <= step - lag < jobs:
            stage2(step - lag)
        if 0 <= step - 2 * lag < jobs:
            stage3(step - 2 * lag)
        if step % 2 == 0 and step // 2 < len(swaps):
            small(step // 2)
    for i in range((jobs + 2 * lag + 1) // 2, len(swaps)):
        small(i)

    for j, (part, slot) in enumerate(kinds):
        for t in range(tp):
            if part is None:
                @pl.when(z != t)
                def _():
                    remote(piece_heads[slot].at[t], last_heads[slot].at[z], s4.at[j, t], r4.at[len(units) + slot, z], {"tp": t}).wait_send()
                    remote(piece_heads[slot].at[t], last_heads[slot].at[t], s4.at[j, t], r4.at[len(units) + slot, t], {"tp": t}).wait_recv()
            elif t == part:
                @pl.when(z != t)
                def _():
                    remote(send3[j], last_units[slot].at[z], s4.at[j, t], r4.at[slot, z], {"tp": t}).wait_send()

                @pl.when(z == t)
                def _():
                    for other in range(tp):
                        if other != t:
                            remote(send3[j], last_units[slot].at[other], s4.at[j, t], r4.at[slot, other], {"tp": t}).wait_recv()
                    last_units[slot][t] = send3[j][...]
    for slot in heads:
        last_heads[slot][z] = piece_heads[slot][z]
    for slots, last, out in ((units, last_units, out_units), (heads, last_heads, out_heads)):
        for slot in slots:

            def body(r, last=last, out=out, slot=slot):
                total = last[slot][0, r].astype(F32)
                for t in range(1, tp):
                    total = total + last[slot][t, r].astype(F32)
                out[slot][r] = total

            rows_loop(out[slot].shape[0], body)
    for k in range(tp if moved else 0):
        @pl.when(z != k)
        def _():
            remote(gt.at[k], gt_out.at[z], sg.at[k], rg.at[z], {"tp": k}).wait_send()
            remote(gt.at[k], gt_out.at[k], sg.at[k], rg.at[k], {"tp": k}).wait_recv()

        @pl.when(z == k)
        def _():
            pltpu.make_async_copy(gt.at[k], gt_out.at[z], lg).wait()


def closing(unit_grads, head_grads, vector, token_grads, tp):
    kinds, operands = [], []
    for t in range(tp if unit_grads else 0):
        for slot, parts in enumerate(unit_grads):
            kinds.append((t, slot))
            operands.append(parts[t])
    for slot, grad in enumerate(head_grads):
        kinds.append((None, slot))
        operands.append(grad)
    operands = [g.reshape((2, 2, 2, g.shape[0] // 8, g.shape[1])) for g in operands]
    rows = operands[0].shape[3]
    jobs = len(kinds)
    vmem, hbm = pl.BlockSpec(memory_space=pltpu.VMEM), pl.BlockSpec(memory_space=pl.ANY)
    heads_w = head_grads[0].shape[1] // tp
    units_w = unit_grads[0][0].shape[1] if unit_grads else 0
    out_shape = (
        [jax.ShapeDtypeStruct((rows, units_w), F32)] * len(unit_grads)
        + [jax.ShapeDtypeStruct((rows, heads_w), F32)] * len(head_grads)
        + [jax.ShapeDtypeStruct(vector.shape, F32), jax.ShapeDtypeStruct(token_grads.shape, token_grads.dtype)]
        + [jax.ShapeDtypeStruct((2, 2, rows, g.shape[-1]), BF16) for g in operands]
    )
    out_specs = [vmem] * (len(unit_grads) + len(head_grads) + 1) + [hbm] * (1 + jobs)
    widths = [g.shape[-1] for g in operands]
    scratch = [pltpu.VMEM((2, 2, 2, rows, w), BF16) for w in sorted(set(widths)) for _ in range(2)]
    scratch += [pltpu.VMEM((2, rows, w), BF16) for w in widths] * 3
    scratch += [pltpu.VMEM((rows, w), BF16) for w in widths] * 2
    scratch += [pltpu.VMEM((tp, rows, units_w), BF16)] * len(unit_grads)
    scratch += [pltpu.VMEM((tp, rows, heads_w), BF16)] * (2 * len(head_grads))
    swaps = 3 + bits_of(tp)
    scratch += [pltpu.VMEM((swaps,) + vector.shape, F32)]
    scratch += [pltpu.SemaphoreType.DMA((jobs,))] * 8
    scratch += [pltpu.SemaphoreType.DMA((jobs, tp)), pltpu.SemaphoreType.DMA((len(unit_grads) + len(head_grads), tp))]
    scratch += [pltpu.SemaphoreType.DMA((swaps,))] * 2 + [pltpu.SemaphoreType.DMA((tp,))] * 2 + [pltpu.SemaphoreType.DMA]
    outs = pl.pallas_call(
        lambda *refs: closing_kernel(kinds, True, tp, refs),
        out_shape=out_shape,
        in_specs=[hbm] * jobs + [vmem, hbm],
        out_specs=out_specs,
        scratch_shapes=scratch,
        compiler_params=pltpu.CompilerParams(collective_id=1, has_side_effects=True, vmem_limit_bytes=62 << 20),
        name="closing",
    )(*operands, vector, token_grads)
    n_u, n_h = len(unit_grads), len(head_grads)
    return outs[:n_u], outs[n_u : n_u + n_h], outs[n_u + n_h], outs[n_u + n_h + 1]


def shards(
    sizes,
    tokens,
    picture,
    ln1_gain,
    ln1_bias,
    w_query,
    b_query,
    w_key,
    w_value,
    b_value,
    w_output,
    b_output,
    ln2_gain,
    ln2_bias,
    w_first,
    b_first,
    w_second,
    b_second,
    cotangent,
):
    tp, ctx = sizes["tp"], sizes["ctx"]
    rows, span, width = tokens.shape
    group = tp // rows
    place = lax.axis_index("tp")
    mine = place % rows
    row = place // group
    part = place % group

    def out_permutation(k):
        return [(s * rows + j, ((j + k) % rows) * group + s) for s in range(group) for j in range(rows)]

    def gather_row(blocks):
        got = []
        for k in range(rows):
            piece = lax.dynamic_index_in_dim(blocks, (mine + k) % rows, 0, keepdims=False)
            pairs = out_permutation(k)
            if any(a != b for a, b in pairs):
                piece = lax.ppermute(piece, "tp", pairs)
            got.append(piece)
        return got

    def scatter_row(values):
        out = jnp.zeros((rows,) + values[0].shape, values[0].dtype)
        for k in range(rows):
            piece = values[k]
            pairs = [(b, a) for a, b in out_permutation(k)]
            if any(a != b for a, b in pairs):
                piece = lax.ppermute(piece, "tp", pairs)
            out = lax.dynamic_update_index_in_dim(out, piece, (mine + k) % rows, 0)
        return out

    def in_order(pieces):
        out = jnp.zeros((rows,) + pieces[0].shape, pieces[0].dtype)
        for k in range(rows):
            out = lax.dynamic_update_index_in_dim(out, pieces[k], (place - k) % rows, 0)
        return out.reshape((-1,) + pieces[0].shape[1:])

    def peers(step):
        s_step, c_step = step % group, step // group
        return s_step, c_step

    def fetch(value, step):
        s_step, c_step = peers(step)
        if s_step:
            pairs = [(r * group + (s + s_step) % group, r * group + s) for r in range(rows) for s in range(group)]
            value = lax.ppermute(value, "tp", pairs)
        if c_step:
            value = lax.ppermute(value, "ctx", [((c + c_step) % ctx, c) for c in range(ctx)])
        return value

    def give(value, step):
        s_step, c_step = peers(step)
        if s_step:
            pairs = [(r * group + s, r * group + (s + s_step) % group) for r in range(rows) for s in range(group)]
            value = lax.ppermute(value, "tp", pairs)
        if c_step:
            value = lax.ppermute(value, "ctx", [(c, (c + c_step) % ctx) for c in range(ctx)])
        return value

    steps = group * ctx

    heads_dev, units = w_query.shape[1], w_first.shape[1]
    both = ("tp", "fsdp")
    shard = jnp.concatenate([w_query, w_key, w_value, w_output.T], axis=1)
    paired = sizes["fsdp"] == 4 and ctx == 2 and group == 1 and bits_of(tp)
    if paired:
        x_all16, qkvo, both_ff = opening(tokens, shard, jnp.stack([w_first, w_second.T]), tp)
        both_ff = both_ff.reshape(2, tp, width, units)
        x_all16 = x_all16.reshape(2 * rows * span, width)
    else:
        first = lax.all_gather(w_first, both, axis=0, tiled=True).reshape(tp, width, units)
        second = lax.all_gather(w_second.T, both, axis=0, tiled=True).reshape(tp, width, units)
        qkvo = lax.all_gather(shard, both, axis=0, tiled=True).reshape(tp, width, 4, heads_dev)
        qkvo = qkvo.transpose(2, 0, 3, 1).reshape(4, tp * heads_dev, width)
        x16 = jnp.concatenate(gather_row(tokens), axis=0)
        x_all16 = jnp.concatenate([x16] + [fetch(x16, i) for i in range(1, steps)], axis=0)
    wq, wkv, wo = qkvo[0], qkvo[1:3].reshape(2 * tp * heads_dev, width), qkvo[3]
    count = rows * span
    ids = lax.dynamic_index_in_dim(picture, row, 0, keepdims=False).reshape(tp, span)
    if not paired:
        order = part * rows + (row - jnp.arange(rows)) % rows
        ids = jnp.take(ids, order, axis=0)
    ids = ids.reshape(count)
    cotangent, x_all16 = lax.optimization_barrier((cotangent, x_all16))
    cot = gather_row(cotangent)
    if paired:
        cot = in_order(cot)
    else:
        cot = jnp.concatenate(cot, axis=0)
    kid = jnp.concatenate([ids] + [fetch(ids, i) for i in range(1, steps)], axis=0)
    block = 256 if count % 256 == 0 else count
    blocks, index = active_blocks(ids, kid, block, block)
    numbers = jnp.arange(8)[:, None]
    qm = jnp.where((numbers < PICS) & (ids[None, :] != numbers), NEG, 0.0).astype(F32)
    km = (kid[None, :] == numbers).astype(F32)

    x_all = x_all16.astype(F32)
    scaled_all, inverse_all = norm_stats(x_all)
    n1 = (scaled_all * ln1_gain + ln1_bias).astype(BF16)
    qt = ((dot(wq, n1[:count], 1, 1) + b_query[:, None]) * (HD ** (-0.5) * LOG2E)).astype(BF16)
    kv_bias = jnp.concatenate([jnp.zeros_like(b_value), b_value])
    kvt = (dot(wkv, n1, 1, 1) + kv_bias[:, None]).astype(BF16)
    ot, lse = attention_forward(blocks, index, qt, kvt, qm, km, block)
    h = x_all[:count] + (dot(ot, wo, 0, 0) + b_output)

    scaled2, inverse2 = norm_stats(h)
    n2 = (scaled2 * ln2_gain + ln2_bias).astype(BF16)
    if paired:
        y, d_n2, g_first, g_second, g_bf = feed(n2, cot, b_first.reshape(tp, 1, units), both_ff, tp)
        g_bf = g_bf.reshape(-1)
        y = h + b_second + y
    else:
        y = h + b_second
        d_n2 = jnp.zeros_like(h)
        g_first, g_second, g_first_bias = [], [], []
        for t in range(tp):
            pre = dot(n2, first[t], 1, 0) + b_first[t * units : (t + 1) * units]
            value, slope = gelu_pair(pre)
            act = value.astype(BF16)
            y = y + dot(act, second[t], 1, 1)
            d_pre = (dot(cot, second[t], 1, 0) * slope).astype(BF16)
            d_n2 = d_n2 + dot(d_pre, first[t], 1, 1)
            g_second.append(dot(cot, act, 0, 0).astype(BF16))
            g_first.append(dot(n2, d_pre, 0, 0).astype(BF16))
            g_first_bias.append(jnp.sum(d_pre.astype(F32), axis=0))
        g_bf = jnp.concatenate(g_first_bias)
    output = y.astype(BF16)
    if paired:
        output = output.reshape(rows, span, width)
        output = scatter_row([lax.dynamic_index_in_dim(output, (place - k) % rows, 0, False) for k in range(rows)])
    else:
        output = scatter_row([output[k * span : (k + 1) * span] for k in range(rows)])
    cot32 = cot.astype(F32)
    g_g2 = jnp.sum(d_n2 * scaled2, axis=0)
    g_c2 = jnp.sum(d_n2, axis=0)
    d_h = cot32 + norm_back(d_n2, scaled2, inverse2, ln2_gain)
    g_bs = jnp.sum(cot32, axis=0)

    d_att = d_h.astype(BF16)
    g_bo = jnp.sum(d_att.astype(F32), axis=0)
    d_ot = dot(wo, d_att, 1, 1).astype(BF16)
    dqt, dkt, dvt = attention_backward(blocks, index, qt, kvt, d_ot, ot, lse, qm, km, block)
    d_all = dot(dkt, wkv[: tp * heads_dev], 0, 0) + dot(dvt, wkv[tp * heads_dev :], 0, 0)
    d_n1 = d_all[:count] + dot(dqt, wq, 0, 0)
    for i in range(1, steps):
        d_n1 = d_n1 + give(d_all[i * count : (i + 1) * count].astype(BF16), i).astype(F32)
    g_query = dot(n1[:count], dqt, 0, 1)
    g_key = dot(n1, dkt, 0, 1)
    g_value = dot(n1, dvt, 0, 1)
    g_out = dot(d_att, ot, 0, 1)
    g_bq = jnp.sum(dqt.astype(F32), axis=1)
    g_bv = jnp.sum(dvt.astype(F32), axis=1)

    scaled1, inverse1 = scaled_all[:count], inverse_all[:count]
    g_g1 = jnp.sum(d_n1 * scaled1, axis=0)
    g_c1 = jnp.sum(d_n1, axis=0)
    grad_tokens = (d_h + norm_back(d_n1, scaled1, inverse1, ln1_gain)).astype(BF16)
    small = [g_g1, g_c1, g_bq, g_bv, g_bo, g_g2, g_c2, g_bf, g_bs]
    vector = jnp.concatenate(small)
    vector = jnp.pad(vector, (0, -vector.shape[0] % 1024)).reshape(-1, 128)
    head_grads = [g.astype(BF16) for g in (g_query, g_key, g_value, g_out)]
    if paired:
        _, heads_out, vector, grad_tokens = closing(
            [], head_grads, vector, grad_tokens.reshape(rows, span, width), tp
        )
        g_query, g_key, g_value, g_out = heads_out
    else:
        g_first, g_second = (
            scatter_units([halve(g, sizes, i % 2 == 0) for g in parts], tp)
            for i, parts in enumerate((g_first, g_second))
        )
        halved = [halve(g, sizes, i % 2 == 0) for i, g in enumerate(head_grads)]
        g_query, g_key, g_value, g_out = (
            scatter_units([g[:, t * heads_dev : (t + 1) * heads_dev] for t in range(tp)], tp) for g in halved
        )
        vector = butterfly(vector, sizes)
        grad_tokens = scatter_row([grad_tokens[k * span : (k + 1) * span] for k in range(rows)])
    grad_tokens = grad_tokens.astype(F32)
    g_out, g_second = g_out.T, g_second.T
    vector = vector.reshape(-1)
    ends = [sum(p.shape[0] for p in small[:i]) for i in range(len(small) + 1)]
    g_g1, g_c1, g_bq, g_bv, g_bo, g_g2, g_c2, g_bf, g_bs = (vector[i:j] for i, j in zip(ends, ends[1:]))
    return (
        output, grad_tokens, g_g1, g_c1, g_query, g_bq, g_key, g_value, g_bv, g_out, g_bo,
        g_g2, g_c2, g_first, g_bf, g_second, g_bs,
    )


def solution(mesh):
    rows_spec = P("fsdp", ("ctx", "tp"), None)
    column, line = P("fsdp", "tp"), P("tp", "fsdp")
    column_out, line_out = P(("fsdp", "ctx"), "tp"), P("tp", ("fsdp", "ctx"))
    return jax.shard_map(
        functools.partial(shards, dict(mesh.shape)),
        mesh=mesh,
        in_specs=(
            rows_spec, P("fsdp", "ctx"), P(), P(), column, P(), column, column, P(), line, P(),
            P(), P(), column, P(), line, P(), rows_spec,
        ),
        out_specs=(
            rows_spec, rows_spec, P(), P(), column_out, P(), column_out, column_out, P(), line_out,
            P(), P(), P(), column_out, P(), line_out, P(),
        ),
        check_vma=False,
    )
```

```python
import functools

import jax
import jax.numpy as jnp
from jax import lax
from jax.experimental import pallas as pl
from jax.experimental.pallas import tpu as pltpu
from jax.sharding import PartitionSpec as P

HD = 72
PICS = 4
EPSILON = 1e-06
LOG2E = 1.4426950408889634
NEG = -1e30
F32 = jnp.float32
BF16 = jnp.bfloat16
MESH = pl.DeviceIdType.MESH


def dot(left, right, left_dim, right_dim):
    return lax.dot_general(
        left, right, (((left_dim,), (right_dim,)), ((), ())), preferred_element_type=F32
    )


def load_augmented(h, q_ref, k_ref, qm_ref, km_ref, kt, qa):
    rows = slice(h * HD, (h + 1) * HD)
    kt[h] = jnp.concatenate([k_ref[rows, :].astype(F32), km_ref[...]], axis=0).T.astype(BF16)
    qa[h] = jnp.concatenate([q_ref[rows, :].astype(F32), qm_ref[...]], axis=0).astype(BF16)


def forward_kernel(nq, nk, block, heads, count, index, q_ref, k_ref, v_ref, qm_ref, km_ref, o_ref, lse_ref, kt, qa):
    for h in range(heads):
        load_augmented(h, q_ref, k_ref, qm_ref, km_ref, kt, qa)
    for qb in range(nq):
        cols = pl.ds(qb * block, block)
        q = [qa[h, :, cols] for h in range(heads)]

        def body(n, carry):
            off = pl.multiple_of(index[qb * nk + n] * block, block)
            scores = [dot(kt[h, pl.ds(off, block), :], q[h], 1, 0) for h in range(heads)]
            out = []
            for h in range(heads):
                top, total, acc = carry[h]
                new = jnp.maximum(top, jnp.max(scores[h], axis=0, keepdims=True))
                p = jnp.exp2(scores[h] - new)
                alpha = jnp.exp2(top - new)
                total = total * alpha + jnp.sum(p, axis=0, keepdims=True)
                acc = acc * alpha + dot(v_ref[h * HD : (h + 1) * HD, pl.ds(off, block)], p.astype(BF16), 1, 0)
                out.append((new, total, acc))
            return tuple(out)

        start = (jnp.full((1, block), 4 * NEG, F32), jnp.zeros((1, block), F32), jnp.zeros((HD, block), F32))
        done = lax.fori_loop(0, count[qb], body, (start,) * heads)
        for h in range(heads):
            top, total, acc = done[h]
            o_ref[h * HD : (h + 1) * HD, cols] = (acc / total).astype(BF16)
            lse_ref[h, :, cols] = top + jnp.log2(total)


def backward_kernel(
    nq, nk, block, heads, count, index, q_ref, k_ref, v_ref, do_ref, o_ref, lse_ref, qm_ref, km_ref,
    dq_ref, dk_ref, dv_ref, kt, vt, qa, dk_acc, dv_acc
):
    for h in range(heads):
        load_augmented(h, q_ref, k_ref, qm_ref, km_ref, kt, qa)
        vt[h] = v_ref[h * HD : (h + 1) * HD, :].astype(F32).T.astype(BF16)
    dk_acc[...] = jnp.zeros_like(dk_acc)
    dv_acc[...] = jnp.zeros_like(dv_acc)
    for qb in range(nq):
        cols = pl.ds(qb * block, block)
        lines = [slice(h * HD, (h + 1) * HD) for h in range(heads)]
        q = [qa[h, :, cols] for h in range(heads)]
        do = [do_ref[lines[h], cols] for h in range(heads)]
        lse = [lse_ref[h, :, cols] for h in range(heads)]
        delta = [
            jnp.sum(do[h].astype(F32) * o_ref[lines[h], cols].astype(F32), axis=0, keepdims=True)
            for h in range(heads)
        ]

        def body(n, carry):
            rows = pl.ds(pl.multiple_of(index[qb * nk + n] * block, block), block)
            scores = [dot(kt[h, rows, :], q[h], 1, 0) for h in range(heads)]
            d_probs = [dot(vt[h, rows, :], do[h], 1, 0) for h in range(heads)]
            out = []
            for h in range(heads):
                p = jnp.exp2(scores[h] - lse[h])
                ds = (p * (d_probs[h] - delta[h])).astype(BF16)
                dv_acc[h, :, rows] += dot(do[h], p.astype(BF16), 1, 1)
                dk_acc[h, :, rows] += dot(q[h][:HD], ds, 1, 1)
                out.append(carry[h] + dot(k_ref[lines[h], rows], ds, 1, 0))
            return tuple(out)

        dq = lax.fori_loop(0, count[qb], body, (jnp.zeros((HD, block), F32),) * heads)
        for h in range(heads):
            dq_ref[lines[h], cols] = (dq[h] * HD ** (-0.5)).astype(BF16)
    for h in range(heads):
        dk_ref[h * HD : (h + 1) * HD, :] = (dk_acc[h] * (1.0 / LOG2E)).astype(BF16)
        dv_ref[h * HD : (h + 1) * HD, :] = dv_acc[h].astype(BF16)


def attention_specs(tokens, context, total, heads):
    q_spec = pl.BlockSpec((HD * heads, tokens), lambda h, *_: (h, 0))
    k_spec = pl.BlockSpec((HD * heads, context), lambda h, *_: (h, 0))
    v_spec = pl.BlockSpec((HD * heads, context), lambda h, *_: (total // heads + h, 0))
    lse_spec = pl.BlockSpec((heads, 1, tokens), lambda h, *_: (h, 0, 0))
    masks = [pl.BlockSpec((8, tokens), lambda h, *_: (0, 0)), pl.BlockSpec((8, context), lambda h, *_: (0, 0))]
    return q_spec, k_spec, v_spec, lse_spec, masks


def attention_forward(count, index, qt, kvt, qm, km, block, heads=8):
    width, tokens = qt.shape
    context, total = kvt.shape[1], width // HD
    q_spec, k_spec, v_spec, lse_spec, masks = attention_specs(tokens, context, total, heads)
    return pl.pallas_call(
        functools.partial(forward_kernel, tokens // block, context // block, block, heads),
        out_shape=(
            jax.ShapeDtypeStruct((width, tokens), BF16),
            jax.ShapeDtypeStruct((total, 1, tokens), F32),
        ),
        grid_spec=pltpu.PrefetchScalarGridSpec(
            num_scalar_prefetch=2,
            grid=(total // heads,),
            in_specs=[q_spec, k_spec, v_spec] + masks,
            out_specs=(q_spec, lse_spec),
            scratch_shapes=[pltpu.VMEM((heads, context, HD + 8), BF16), pltpu.VMEM((heads, HD + 8, tokens), BF16)],
        ),
        compiler_params=pltpu.CompilerParams(vmem_limit_bytes=56 << 20),
        cost_estimate=pl.CostEstimate(
            flops=tokens * context * width * 12, bytes_accessed=width * (tokens + context) * 4,
            transcendentals=tokens * context * total // 2,
        ),
        name="attention_forward",
    )(count, index, qt, kvt, kvt, qm, km)


def attention_backward(count, index, qt, kvt, d_ot, ot, lse, qm, km, block, heads=8):
    width, tokens = qt.shape
    context, total = kvt.shape[1], width // HD
    q_spec, k_spec, v_spec, lse_spec, masks = attention_specs(tokens, context, total, heads)
    return pl.pallas_call(
        functools.partial(backward_kernel, tokens // block, context // block, block, heads),
        out_shape=(
            jax.ShapeDtypeStruct((width, tokens), BF16),
            jax.ShapeDtypeStruct((width, context), BF16),
            jax.ShapeDtypeStruct((width, context), BF16),
        ),
        grid_spec=pltpu.PrefetchScalarGridSpec(
            num_scalar_prefetch=2,
            grid=(total // heads,),
            in_specs=[q_spec, k_spec, v_spec, q_spec, q_spec, lse_spec] + masks,
            out_specs=(q_spec, k_spec, k_spec),
            scratch_shapes=[
                pltpu.VMEM((heads, context, HD + 8), BF16),
                pltpu.VMEM((heads, context, HD), BF16),
                pltpu.VMEM((heads, HD + 8, tokens), BF16),
                pltpu.VMEM((heads, HD, context), F32),
                pltpu.VMEM((heads, HD, context), F32),
            ],
        ),
        compiler_params=pltpu.CompilerParams(vmem_limit_bytes=56 << 20),
        cost_estimate=pl.CostEstimate(
            flops=tokens * context * width * 20, bytes_accessed=width * (tokens + context) * 8,
            transcendentals=tokens * context * total // 2,
        ),
        name="attention_backward",
    )(count, index, qt, kvt, kvt, d_ot, ot, lse, qm, km)


def active_blocks(qid, kid, bq, bk):
    q = qid.reshape(-1, bq)
    k = kid.reshape(-1, bk)
    q_low, q_high = jnp.min(q, 1)[:, None], jnp.max(q, 1)[:, None]
    k_low, k_high = jnp.min(k, 1)[None, :], jnp.max(k, 1)[None, :]
    active = (q_low <= k_high) & (k_low <= q_high)
    slots = jnp.arange(k.shape[0], dtype=jnp.int32)
    before = (slots[:, None] < slots[None, :])[None]
    place = jnp.sum((active[:, :, None] & before).astype(jnp.int32), axis=1)
    hit = active[:, None, :] & (place[:, None, :] == slots[None, :, None])
    index = jnp.sum(jnp.where(hit, slots[None, None, :], 0), axis=2)
    return jnp.sum(active.astype(jnp.int32), axis=1), index.reshape(-1)


def norm_stats(values):
    centred = values - jnp.mean(values, axis=-1, keepdims=True)
    inverse = lax.rsqrt(jnp.mean(centred * centred, axis=-1, keepdims=True) + EPSILON)
    return centred * inverse, inverse


def norm_back(grad, scaled, inverse, gain):
    wide = grad * gain
    return inverse * (
        wide
        - jnp.mean(wide, axis=-1, keepdims=True)
        - scaled * jnp.mean(wide * scaled, axis=-1, keepdims=True)
    )


def gelu_pair(pre):
    c = 0.7978845608028654
    square = pre * pre
    t = jnp.tanh(c * pre * (1.0 + 0.044715 * square))
    value = 0.5 * pre * (1.0 + t)
    slope = 0.5 * (1.0 + t) + 0.5 * pre * (1.0 - t * t) * c * (1.0 + 3 * 0.044715 * square)
    return value, slope


def bits_of(size):
    assert size & (size - 1) == 0
    return size.bit_length() - 1


def exchange(value, axis, size, flip):
    return lax.ppermute(value, axis, [(i, i ^ flip) for i in range(size)])


def butterfly(value, sizes):
    for axis, size in sizes.items():
        for bit in range(bits_of(size)):
            value = value + exchange(value, axis, size, 1 << bit)
    return value


def halve(grad, sizes, ctx_first):
    fsdp, ctx = sizes["fsdp"], sizes["ctx"]
    nf, nc = bits_of(fsdp), bits_of(ctx)
    total = grad.reshape((2,) * (nf + nc) + (-1, grad.shape[-1])).astype(F32)
    f_stages = [("fsdp", fsdp, bit) for bit in range(nf)]
    c_stages = [("ctx", ctx, bit) for bit in range(nc)]
    stages = f_stages[:1] + (c_stages + f_stages[1:] if ctx_first else f_stages[1:] + c_stages)
    left = [("fsdp", bit) for bit in reversed(range(nf))] + [("ctx", bit) for bit in reversed(range(nc))]
    for axis, size, bit in stages:
        dim = left.index((axis, bit))
        mine = (lax.axis_index(axis) >> bit) & 1
        send = lax.dynamic_index_in_dim(total, 1 - mine, dim, keepdims=False).astype(BF16)
        keep = lax.dynamic_index_in_dim(total, mine, dim, keepdims=False)
        total = keep + exchange(send, axis, size, 1 << bit).astype(F32)
        left.pop(dim)
    return total


def scatter_units(parts, tp):
    place = lax.axis_index("tp")
    stack = jnp.stack([p.astype(BF16) for p in parts])
    total = lax.dynamic_index_in_dim(jnp.stack(parts), place, 0, keepdims=False)
    for k in range(1, tp):
        piece = lax.dynamic_index_in_dim(stack, place ^ k, 0, keepdims=False)
        total = total + exchange(piece, "tp", tp, k).astype(F32)
    return total


def opening_kernel(
    tp, tokens, shard, ff_in, x_all, wt, ff, pieces,
    st, rt, sy, ry, sz, rz, sx, rx, sn, rn, own, fsz, frz, fsx, frx, fsy, fry, fsn, frn
):
    f, c, z = lax.axis_index("fsdp"), lax.axis_index("ctx"), lax.axis_index("tp")
    near, across = f + 1 - 2 * (f % 2), f + 2 - 4 * (f // 2)
    other_c = 1 - c

    barrier = pltpu.get_barrier_semaphore()
    for where in ({"fsdp": near}, {"fsdp": across}, {"ctx": other_c}):
        pl.semaphore_signal(barrier, inc=1, device_id=where, device_id_type=MESH)
    for k in range(1, tp):
        pl.semaphore_signal(barrier, inc=1, device_id={"tp": lax.rem(z + k, tp)}, device_id_type=MESH)
    start = pltpu.make_async_copy(shard, pieces.at[z, f], own.at[0])
    start.start()
    mine = [pltpu.make_async_copy(ff_in.at[m], ff.at[m, z, f], own.at[1 + m]) for m in range(2)]
    for copy in mine:
        copy.start()
    start.wait()
    pl.semaphore_wait(barrier, 2 + tp)

    def remote(src, dst, send, recv, where):
        return pltpu.make_async_remote_copy(
            src_ref=src, dst_ref=dst, send_sem=send, recv_sem=recv, device_id=where, device_id_type=MESH
        )

    def along(t, side):
        return remote(pieces.at[t, f], pieces.at[t, f], sz.at[t, side], rz.at[t], {"tp": z + 1 if side else z - 1})

    def cross(t):
        return remote(pieces.at[t, f], pieces.at[t, f], sx.at[t], rx.at[t], {"fsdp": across})

    def beside(t, i):
        source = across if i else f
        return remote(pieces.at[t, source], pieces.at[t, source], sn.at[t, i], rn.at[t, i], {"fsdp": near})

    def token(k, row):
        return remote(tokens.at[k], x_all.at[0, row], st.at[k], rt.at[row], {"tp": k})

    def half(t):
        return remote(x_all.at[0, t], x_all.at[1, t], sy.at[t], ry.at[t], {"ctx": other_c})

    def ff_along(t, side):
        part = ff.at[c, t, f]
        return remote(part, part, fsz.at[t, side], frz.at[t], {"tp": z + 1 if side else z - 1})

    def ff_cross(m, t):
        part = ff.at[m, t, f]
        return remote(part, part, fsx.at[m, t], frx.at[m, t], {"fsdp": across})

    def ff_half(t, i):
        part = ff.at[c, t, across if i else f]
        return remote(part, part, fsy.at[t, i], fry.at[t, i], {"ctx": other_c})

    def ff_beside(m, t, i):
        part = ff.at[m, t, across if i else f]
        return remote(part, part, fsn.at[m, t, i], frn.at[m, t, i], {"fsdp": near})

    def passes(t, right, left):
        @pl.when((t <= z) & (z < tp - 1))
        def _():
            right(t)

        @pl.when((t >= z) & (z > 0))
        def _():
            left(t)

    def onward(t):
        passes(t, lambda t: along(t, 1).start(), lambda t: along(t, 0).start())
        cross(t).start()
        beside(t, 0).start()

    def ff_pass(t):
        passes(t, lambda t: ff_along(t, 1).start(), lambda t: ff_along(t, 0).start())

    def arrivals(d, wait, then):
        for t, there in ((z - d, z >= d), (z + d, z + d < tp)):
            @pl.when(there)
            def _():
                wait(t)
                then(t)

    depth = shard.shape[0]
    columns = shard.shape[1] // 4

    def turn(t):
        for i in range(2):
            beside(t, i).wait_recv()
        for g in range(4):
            for w in range(4):
                piece = pieces[t, g, :, w * columns : (w + 1) * columns].astype(F32).T.astype(BF16)
                wt[w, pl.ds(pl.multiple_of(t * columns, 32), columns), g * depth : (g + 1) * depth] = piece

    def ff_onward(t):
        ff_pass(t)
        ff_cross(c, t).start()
        ff_half(t, 0).start()
        ff_beside(c, t, 0).start()

    def ff_second(t):
        ff_cross(c, t).wait_recv()
        ff_half(t, 1).start()
        ff_beside(c, t, 1).start()

    def handed(t):
        for i in range(2):
            ff_half(t, i).wait_recv()
            ff_beside(1 - c, t, i).start()

    def nothing(t):
        return None

    onward(z)
    local = pltpu.make_async_copy(tokens.at[z], x_all.at[0, z], own.at[0])
    local.start()
    for m in range(2):
        mine[m].wait()
    ff_pass(z)
    for m in range(2):
        ff_cross(m, z).start()
        ff_beside(m, z, 0).start()
    local.wait()
    half(z).start()
    for d in range(1, tp):
        arrivals(d, lambda t: along(t, 0).wait_recv(), onward)
        arrivals(d, lambda t: ff_along(t, 0).wait_recv(), ff_onward)
        if d > 1:
            token(z ^ (d - 1), z).start()
        cross(z ^ (d - 1)).wait_recv()
        beside(z ^ (d - 1), 1).start()
        if d == 1:
            for m in range(2):
                ff_cross(m, z).wait_recv()
                ff_beside(m, z, 1).start()
        else:
            arrivals(d - 1, nothing, ff_second)
    token(z ^ (tp - 1), z).start()
    turn(z)
    cross(z ^ (tp - 1)).wait_recv()
    beside(z ^ (tp - 1), 1).start()
    arrivals(tp - 1, nothing, ff_second)
    turn(z ^ 1)
    arrivals(1, nothing, handed)
    token(z ^ 1, z ^ 1).wait_recv()
    half(z ^ 1).start()
    for d in range(2, tp):
        turn(z ^ d)
        arrivals(d, nothing, handed)
        token(z ^ d, z ^ d).wait_recv()
        half(z ^ d).start()

    for k in range(tp):
        t = z ^ k
        passes(t, lambda t: along(t, 1).wait_send(), lambda t: along(t, 0).wait_send())
        passes(t, lambda t: ff_along(t, 1).wait_send(), lambda t: ff_along(t, 0).wait_send())
        cross(t).wait_send()
        beside(t, 0).wait_send()
        beside(t, 1).wait_send()
        if k:
            token(t, z).wait_send()
        half(t).wait()
        for m in range(2):
            if k == 0:
                ff_cross(m, t).wait_send()
            for i in range(2):
                ff_beside(m, t, i).wait()
        if k:
            ff_cross(c, t).wait_send()
            for i in range(2):
                ff_half(t, i).wait_send()


def opening(tokens, shard, ff_in, tp):
    rows, span, width = tokens.shape
    vmem, hbm = pl.BlockSpec(memory_space=pltpu.VMEM), pl.BlockSpec(memory_space=pl.ANY)
    depth, columns = shard.shape[0], shard.shape[1] // 4
    dma = pltpu.SemaphoreType.DMA
    return pl.pallas_call(
        functools.partial(opening_kernel, tp),
        out_shape=(
            jax.ShapeDtypeStruct((2, rows, span, width), BF16),
            jax.ShapeDtypeStruct((4, tp * columns, 4 * depth), BF16),
            jax.ShapeDtypeStruct((2, tp, 4) + ff_in.shape[1:], BF16),
        ),
        in_specs=[hbm, hbm, hbm],
        out_specs=(hbm, vmem, hbm),
        scratch_shapes=[pltpu.VMEM((tp, 4, depth, 4 * columns), BF16)]
        + [dma((tp,))] * 4
        + [dma((tp, 2)), dma((tp,)), dma((tp,)), dma((tp,)), dma((tp, 2)), dma((tp, 2)), dma((3,))]
        + [dma((tp, 2)), dma((tp,)), dma((2, tp)), dma((2, tp)), dma((tp, 2)), dma((tp, 2))]
        + [dma((2, tp, 2)), dma((2, tp, 2))],
        compiler_params=pltpu.CompilerParams(collective_id=2, has_side_effects=True, vmem_limit_bytes=48 << 20),
        name="opening",
    )(tokens, shard, ff_in)


def turn_rows(source, target, g, depth, core):
    place = g // 2 + 2 * (core if g % 2 else 1 - core)
    rows = pl.ds(pl.multiple_of(place * depth, 32), depth)
    target[rows, :] = source[:, g * depth : (g + 1) * depth].astype(F32).T.astype(BF16)


def feed_kernel(
    tp, n2, cot, bias, ff, y, dn2, g_first, g_second, g_bias,
    n2t, cott, weights, act, d_pre, near_part, recv1, recv2, recv3, recvz,
    lw, s1, r1, s2, r2, s3, r3, s4, r4
):
    f, c, z = lax.axis_index("fsdp"), lax.axis_index("ctx"), lax.axis_index("tp")
    x, core = f // 2, f % 2
    near, across, other_c = f + 1 - 2 * core, f + 2 - 4 * x, 1 - c
    tokens, width = n2.shape
    depth = width // 4
    order = list(range(tp - 1, -1, -1))

    def load(i):
        return [pltpu.make_async_copy(ff.at[m, z ^ order[i]], weights.at[m], lw.at[m]) for m in range(2)]

    for copy in load(0):
        copy.start()

    barrier = pltpu.get_barrier_semaphore()
    for where in ({"fsdp": near}, {"fsdp": across}, {"ctx": other_c}):
        pl.semaphore_signal(barrier, inc=1, device_id=where, device_id_type=MESH)
    for k in range(1, tp):
        pl.semaphore_signal(barrier, inc=1, device_id={"tp": z ^ k}, device_id_type=MESH)

    for g in range(4):
        turn_rows(n2, n2t, g, depth, core)
        turn_rows(cot, cott, g, depth, core)
    pl.semaphore_wait(barrier, 2 + tp)

    def remote(src, dst, send, recv, where):
        return pltpu.make_async_remote_copy(
            src_ref=src, dst_ref=dst, send_sem=send, recv_sem=recv, device_id=where, device_id_type=MESH
        )

    def first(j, m):
        return remote(near_part.at[m], recv1.at[j], s1.at[j], r1.at[j], {"fsdp": near})

    def second(j, m):
        if m == 0:
            return remote(recv1.at[j, 1 - x], recv2.at[j], s2.at[j], r2.at[j], {"fsdp": across})
        return remote(recv1.at[j, :, 1 - c], recv2.at[j], s2.at[j], r2.at[j], {"ctx": other_c})

    def third(j, m):
        if m == 0:
            return remote(recv2.at[j, 1 - c], recv3.at[j], s3.at[j], r3.at[j], {"ctx": other_c})
        return remote(recv2.at[j, 1 - x], recv3.at[j], s3.at[j], r3.at[j], {"fsdp": across})

    def last(j, m, k):
        return remote(recv3.at[j], recvz.at[m, k - 1], s4.at[m, k - 1], r4.at[m, k - 1], {"tp": z ^ k})

    half = depth // 2
    tile = 48

    def stage2(i):
        for m in range(2):
            j = 2 * i + m
            second(j, m).wait()

            @pl.loop(0, half // tile)
            def _(n):
                r = pl.ds(pl.multiple_of(n * tile, 16), tile)
                for a in range(2):
                    kept = recv1[j, x, a, r] if m == 0 else recv1[j, a, c, r]
                    recv2[j, a, r] = (kept.astype(F32) + recv2[j, a, r].astype(F32)).astype(BF16)

            third(j, m).start()

    def stage3(i):
        for m in range(2):
            j = 2 * i + m
            third(j, m).wait()

            @pl.loop(0, half // tile)
            def _(n):
                r = pl.ds(pl.multiple_of(n * tile, 16), tile)
                recv3[j, r] = (recv2[j, c if m == 0 else x, r].astype(F32) + recv3[j, r].astype(F32)).astype(BF16)

            if order[i]:
                last(j, m, order[i]).start()

    rows_tile = 512
    sides = ((n2t, d_pre), (cott, act))

    def sums(first_time, which):
        @pl.loop(0, tokens // rows_tile)
        def _(n):
            r = pl.ds(pl.multiple_of(n * rows_tile, rows_tile), rows_tile)
            for total, left, m in ((y, act, 1), (dn2, d_pre, 0)):
                if m in which:
                    part = dot(left[r, :], weights[m], 1, 1)
                    total[r, :] = part if first_time else total[r, :] + part

    def own_part(i):
        for m, (left, right) in enumerate(sides):
            j = 2 * i + m
            first(j, m).wait_recv()

            grad = dot(left[2 * depth :, :], right[...], 1, 0)
            for n in range(4):
                a, b = divmod(n, 2)
                recv1[j, a, b] = (grad[n * half : (n + 1) * half] + recv1[j, a, b].astype(F32)).astype(BF16)

            second(j, m).start()

    for i in range(tp):
        for copy in load(i):
            copy.wait()
        t = z ^ order[i]
        g_bias[t] = jnp.zeros_like(g_bias[t])

        @pl.loop(0, tokens // rows_tile)
        def _(n):
            r = pl.ds(pl.multiple_of(n * rows_tile, rows_tile), rows_tile)
            value, slope = gelu_pair(dot(n2[r, :], weights[0], 1, 0) + bias[t])
            act[r, :] = value.astype(BF16)
            back = (dot(cot[r, :], weights[1], 1, 0) * slope).astype(BF16)
            d_pre[r, :] = back
            g_bias[t] += jnp.sum(back.astype(F32), axis=0, keepdims=True)

        for m, (left, right) in enumerate(sides):
            j = 2 * i + m
            if i:
                first(j - 2, m).wait_send()

            grad = dot(left[: 2 * depth, :], right[...], 1, 0).astype(BF16)
            for n in range(4):
                near_part[m, n // 2, n % 2] = grad[n * half : (n + 1) * half]

            first(j, m).start()
        if i:
            stage2(i - 1)
        if i + 1 < tp:
            sums(i == 0, (0, 1))
            for copy in load(i + 1):
                copy.start()
            if i:
                stage3(i - 1)
            own_part(i)
        else:
            sums(i == 0, (1,))
            if i:
                stage3(i - 1)
            own_part(i)
            sums(i == 0, (0,))
    stage2(tp - 1)
    stage3(tp - 1)
    for m, out in enumerate((g_first, g_second)):
        first(2 * (tp - 1) + m, m).wait_send()
        for k in range(1, tp):
            last(2 * (tp - 1 - k) + m, m, k).wait()

        @pl.loop(0, half // tile)
        def _(n):
            r = pl.ds(pl.multiple_of(n * tile, 16), tile)
            total = recv3[2 * (tp - 1) + m, r].astype(F32)
            for k in range(1, tp):
                total = total + recvz[m, k - 1, r].astype(F32)
            out[r] = total


def feed(n2, cot, bias, ff, tp):
    tokens, width = n2.shape
    units, half = ff.shape[-1], width // 8
    vmem, hbm = pl.BlockSpec(memory_space=pltpu.VMEM), pl.BlockSpec(memory_space=pl.ANY)
    dma = pltpu.SemaphoreType.DMA
    return pl.pallas_call(
        functools.partial(feed_kernel, tp),
        out_shape=(
            jax.ShapeDtypeStruct((tokens, width), F32),
            jax.ShapeDtypeStruct((tokens, width), F32),
            jax.ShapeDtypeStruct((half, units), F32),
            jax.ShapeDtypeStruct((half, units), F32),
            jax.ShapeDtypeStruct((tp, 1, units), F32),
        ),
        in_specs=[vmem, vmem, vmem, hbm],
        out_specs=(vmem,) * 5,
        scratch_shapes=[
            pltpu.VMEM((width, tokens), BF16),
            pltpu.VMEM((width, tokens), BF16),
            pltpu.VMEM((2, width, units), BF16),
            pltpu.VMEM((tokens, units), BF16),
            pltpu.VMEM((tokens, units), BF16),
            pltpu.VMEM((2, 2, 2, half, units), BF16),
            pltpu.VMEM((2 * tp, 2, 2, half, units), BF16),
            pltpu.VMEM((2 * tp, 2, half, units), BF16),
            pltpu.VMEM((2 * tp, half, units), BF16),
            pltpu.VMEM((2, tp - 1, half, units), BF16),
            dma((2,)),
        ]
        + [dma((2 * tp,))] * 6
        + [dma((2, tp - 1))] * 2,
        compiler_params=pltpu.CompilerParams(collective_id=3, has_side_effects=True, vmem_limit_bytes=63 << 20),
        cost_estimate=pl.CostEstimate(
            flops=12 * tokens * width * tp * units, bytes_accessed=4 * width * tp * units + 16 * tokens * width,
            transcendentals=tokens * tp * units,
        ),
        name="feed",
    )(n2, cot, bias, ff)


def closing_kernel(
    tp, d_other, d_own, d_h, x_own, n1, d_att, gain, dqt, dkt, dvt, ot, vec,
    g_q, g_k, g_v, g_o, vec_out, gt_out,
    n1t, d_att_t, stage, come, block_a, block_b, block_x, gt, g_gain, g_bias, near_part, recv1, recv2, recv3, piece, recvz, vec_in,
    sy, ry, lb, sg, rg, lg, ls, s1, r1, s2, r2, s3, r3, s4, r4, sv, rv
):
    f, c, z = lax.axis_index("fsdp"), lax.axis_index("ctx"), lax.axis_index("tp")
    x, core = f // 2, f % 2
    near, across, other_c = f + 1 - 2 * core, f + 2 - 4 * x, 1 - c
    span, width = come.shape[1:]
    tokens = tp * span
    depth = width // 4
    half = depth // 2
    tile = 48
    order = list(range(tp - 1, -1, -1))

    def loads(i):
        b, slot = z ^ order[i], i % 2
        return [
            pltpu.make_async_copy(source.at[b], target.at[slot], lb.at[n, slot])
            for n, (source, target) in enumerate(((d_own, block_a), (d_h, block_b), (x_own, block_x)))
        ]

    for copy in loads(0):
        copy.start()

    barrier = pltpu.get_barrier_semaphore()
    for where in ({"fsdp": near}, {"fsdp": across}, {"ctx": other_c}):
        pl.semaphore_signal(barrier, inc=1, device_id=where, device_id_type=MESH)
    for k in range(1, tp):
        pl.semaphore_signal(barrier, inc=1, device_id={"tp": z ^ k}, device_id_type=MESH)
    pl.semaphore_wait(barrier, 2 + tp)

    def remote(src, dst, send, recv, where):
        return pltpu.make_async_remote_copy(
            src_ref=src, dst_ref=dst, send_sem=send, recv_sem=recv, device_id=where, device_id_type=MESH
        )

    def over(k):
        return remote(d_other.at[z ^ k], come.at[z ^ k], sy.at[k], ry.at[k], {"ctx": other_c})

    for k in order:
        over(k).start()

    def first(j):
        return remote(near_part.at[j], recv1.at[j], s1.at[j], r1.at[j], {"fsdp": near})

    def second(j):
        return remote(recv1.at[j, 1 - x], recv2.at[j], s2.at[j], r2.at[j], {"fsdp": across})

    def third(j):
        return remote(recv2.at[j, 1 - c], recv3.at[j], s3.at[j], r3.at[j], {"ctx": other_c})

    def last(j, k):
        return remote(piece.at[j, z ^ k], recvz.at[j, k - 1], s4.at[j, k - 1], r4.at[j, k - 1], {"tp": z ^ k})

    def move(k):
        return remote(gt.at[z ^ k], gt_out.at[z], sg.at[k], rg.at[k], {"tp": z ^ k})

    jobs = ((d_att_t, ot, tokens), (n1t, dkt, 2 * tokens), (n1t, dvt, 2 * tokens), (n1t, dqt, tokens))

    def near_side(j):
        left, right, length = jobs[j]
        grad = dot(left[: 2 * depth, :length], right[...], 1, 1).astype(BF16)
        for n in range(4):
            near_part[j, n // 2, n % 2] = grad[n * half : (n + 1) * half]
        first(j).start()

    def own_side(j):
        left, right, length = jobs[j]
        grad = dot(left[2 * depth :, :length], right[...], 1, 1)
        first(j).wait_recv()
        for n in range(4):
            a, b = divmod(n, 2)
            recv1[j, a, b] = (grad[n * half : (n + 1) * half] + recv1[j, a, b].astype(F32)).astype(BF16)
        second(j).start()

    def fetch(source, n, slot):
        rows = pl.ds(pl.multiple_of(n * span, span), span)
        return pltpu.make_async_copy(source.at[rows], stage.at[slot], ls.at[slot])

    def turned(source, target, blocks):
        fetch(source, 0, 0).start()

        @pl.loop(0, blocks)
        def _(n):
            slot = lax.rem(n, 2)

            @pl.when(n + 1 < blocks)
            def _():
                fetch(source, n + 1, 1 - slot).start()

            fetch(source, n, slot).wait()
            cols = pl.ds(pl.multiple_of(n * span, span), span)
            for g in range(4):
                place = g // 2 + 2 * (core if g % 2 else 1 - core)
                rows = pl.ds(pl.multiple_of(place * depth, 32), depth)
                part = stage[slot, :, g * depth : (g + 1) * depth]
                target[rows, cols] = part.astype(F32).T.astype(BF16)

    def stage2(j):
        second(j).wait()

        @pl.loop(0, half // tile)
        def _(n):
            r = pl.ds(pl.multiple_of(n * tile, 16), tile)
            for a in range(2):
                recv2[j, a, r] = (recv1[j, x, a, r].astype(F32) + recv2[j, a, r].astype(F32)).astype(BF16)

        third(j).start()

    def stage3(j):
        third(j).wait()
        columns = width // tp

        @pl.loop(0, half // tile)
        def _(n):
            r = pl.ds(pl.multiple_of(n * tile, 16), tile)
            total = recv2[j, c, r].astype(F32) + recv3[j, r].astype(F32)
            for t in range(tp):
                piece[j, t, r] = total[:, t * columns : (t + 1) * columns].astype(BF16)

        for k in range(1, tp):
            last(j, k).start()

    g_gain[...] = jnp.zeros_like(g_gain)
    g_bias[...] = jnp.zeros_like(g_bias)

    def token_block(i):
        k = order[i]
        b, slot = z ^ k, i % 2
        if i + 1 < tp:
            for copy in loads(i + 1):
                copy.start()
        for copy in loads(i):
            copy.wait()
        over(k).wait()
        lines = 32

        @pl.loop(0, span // lines)
        def _(n):
            r = pl.ds(pl.multiple_of(n * lines, lines), lines)
            scaled, inverse = norm_stats(block_x[slot, r].astype(F32))
            d_n1 = block_a[slot, r] + come[b, r].astype(F32)
            g_gain[...] += jnp.sum(d_n1 * scaled, axis=0, keepdims=True)
            g_bias[...] += jnp.sum(d_n1, axis=0, keepdims=True)
            gt[b, r] = (block_b[slot, r] + norm_back(d_n1, scaled, inverse, gain[...])).astype(BF16)

        if k:
            move(k).start()

    turned(d_att, d_att_t, tp)
    near_side(0)
    own_side(0)
    turned(n1, n1t, 2 * tp)
    near_side(1)
    token_block(0)
    own_side(1)
    near_side(2)
    token_block(1)
    near_side(3)
    own_side(2)
    stage2(0)
    own_side(3)
    for i in range(2, tp):
        token_block(i)
    local = pltpu.make_async_copy(gt.at[z], gt_out.at[z], lg)
    local.start()

    flips = [{"fsdp": near}, {"fsdp": across}, {"ctx": other_c}] + [{"tp": z ^ (1 << i)} for i in range(bits_of(tp))]
    swaps = [remote(vec_out, vec_in.at[i], sv.at[i], rv.at[i], where) for i, where in enumerate(flips)]
    vec_out[...] = vec[...]
    lanes = width // 128
    for n, part in enumerate((g_gain, g_bias)):
        for i in range(lanes):
            vec_out[n * lanes + i : n * lanes + i + 1, :] = part[:, i * 128 : (i + 1) * 128]
    swaps[0].start()

    def small(i):
        swaps[i].wait()
        vec_out[...] = vec_out[...] + vec_in[i]
        if i + 1 < len(swaps):
            swaps[i + 1].start()

    small(0)
    stage2(1)
    stage3(0)
    small(1)
    stage2(2)
    stage3(1)
    small(2)
    stage2(3)
    stage3(2)
    stage3(3)
    for i in range(3, len(swaps)):
        small(i)
    for j, out in enumerate((g_o, g_k, g_v, g_q)):
        first(j).wait_send()
        for k in range(1, tp):
            last(j, k).wait()

        @pl.loop(0, half // tile)
        def _(n):
            r = pl.ds(pl.multiple_of(n * tile, 16), tile)
            total = piece[j, z, r].astype(F32)
            for k in range(1, tp):
                total = total + recvz[j, k - 1, r].astype(F32)
            out[r] = total

    local.wait()
    for k in range(1, tp):
        move(k).wait()


def closing(d_other, d_own, d_h, x_own, n1, d_att, gain, dqt, dkt, dvt, ot, vector, tp):
    context, width = n1.shape
    tokens = context // 2
    span = tokens // tp
    half, columns = width // 8, width // tp
    vmem, hbm = pl.BlockSpec(memory_space=pltpu.VMEM), pl.BlockSpec(memory_space=pl.ANY)
    dma = pltpu.SemaphoreType.DMA
    swaps = 3 + bits_of(tp)
    blocks = [a.reshape(tp, span, width) for a in (d_other, d_own, d_h, x_own)]
    return pl.pallas_call(
        functools.partial(closing_kernel, tp),
        out_shape=[jax.ShapeDtypeStruct((half, columns), F32)] * 4
        + [jax.ShapeDtypeStruct(vector.shape, F32), jax.ShapeDtypeStruct((tp, span, width), BF16)],
        in_specs=[hbm] * 6 + [vmem] * 6,
        out_specs=[vmem] * 5 + [hbm],
        scratch_shapes=[
            pltpu.VMEM((width, context), BF16),
            pltpu.VMEM((width, tokens), BF16),
            pltpu.VMEM((2, span, width), BF16),
            pltpu.VMEM((tp, span, width), BF16),
            pltpu.VMEM((2, span, width), F32),
            pltpu.VMEM((2, span, width), F32),
            pltpu.VMEM((2, span, width), BF16),
            pltpu.VMEM((tp, span, width), BF16),
            pltpu.VMEM((1, width), F32),
            pltpu.VMEM((1, width), F32),
            pltpu.VMEM((4, 2, 2, half, width), BF16),
            pltpu.VMEM((4, 2, 2, half, width), BF16),
            pltpu.VMEM((4, 2, half, width), BF16),
            pltpu.VMEM((4, half, width), BF16),
            pltpu.VMEM((4, tp, half, columns), BF16),
            pltpu.VMEM((4, tp - 1, half, columns), BF16),
            pltpu.VMEM((swaps,) + vector.shape, F32),
            dma((tp,)), dma((tp,)), dma((3, 2)), dma((tp,)), dma((tp,)), dma, dma((2,)),
            dma((4,)), dma((4,)), dma((4,)), dma((4,)), dma((4,)), dma((4,)),
            dma((4, tp - 1)), dma((4, tp - 1)), dma((swaps,)), dma((swaps,)),
        ],
        compiler_params=pltpu.CompilerParams(collective_id=1, has_side_effects=True, vmem_limit_bytes=63 << 20),
        name="closing",
    )(*blocks, n1, d_att, gain, dqt, dkt, dvt, ot, vector)


def shards(
    sizes,
    tokens,
    picture,
    ln1_gain,
    ln1_bias,
    w_query,
    b_query,
    w_key,
    w_value,
    b_value,
    w_output,
    b_output,
    ln2_gain,
    ln2_bias,
    w_first,
    b_first,
    w_second,
    b_second,
    cotangent,
):
    tp, ctx = sizes["tp"], sizes["ctx"]
    rows, span, width = tokens.shape
    group = tp // rows
    place = lax.axis_index("tp")
    mine = place % rows
    row = place // group
    part = place % group

    def out_permutation(k):
        return [(s * rows + j, ((j + k) % rows) * group + s) for s in range(group) for j in range(rows)]

    def gather_row(blocks):
        got = []
        for k in range(rows):
            piece = lax.dynamic_index_in_dim(blocks, (mine + k) % rows, 0, keepdims=False)
            pairs = out_permutation(k)
            if any(a != b for a, b in pairs):
                piece = lax.ppermute(piece, "tp", pairs)
            got.append(piece)
        return got

    def scatter_row(values):
        out = jnp.zeros((rows,) + values[0].shape, values[0].dtype)
        for k in range(rows):
            piece = values[k]
            pairs = [(b, a) for a, b in out_permutation(k)]
            if any(a != b for a, b in pairs):
                piece = lax.ppermute(piece, "tp", pairs)
            out = lax.dynamic_update_index_in_dim(out, piece, (mine + k) % rows, 0)
        return out

    def in_order(pieces):
        out = jnp.zeros((rows,) + pieces[0].shape, pieces[0].dtype)
        for k in range(rows):
            out = lax.dynamic_update_index_in_dim(out, pieces[k], (place - k) % rows, 0)
        return out.reshape((-1,) + pieces[0].shape[1:])

    def peers(step):
        s_step, c_step = step % group, step // group
        return s_step, c_step

    def fetch(value, step):
        s_step, c_step = peers(step)
        if s_step:
            pairs = [(r * group + (s + s_step) % group, r * group + s) for r in range(rows) for s in range(group)]
            value = lax.ppermute(value, "tp", pairs)
        if c_step:
            value = lax.ppermute(value, "ctx", [((c + c_step) % ctx, c) for c in range(ctx)])
        return value

    def give(value, step):
        s_step, c_step = peers(step)
        if s_step:
            pairs = [(r * group + s, r * group + (s + s_step) % group) for r in range(rows) for s in range(group)]
            value = lax.ppermute(value, "tp", pairs)
        if c_step:
            value = lax.ppermute(value, "ctx", [(c, (c + c_step) % ctx) for c in range(ctx)])
        return value

    steps = group * ctx

    heads_dev, units = w_query.shape[1], w_first.shape[1]
    padding = -units % 128
    both = ("tp", "fsdp")
    shard = jnp.concatenate([w_query, w_key, w_value, w_output.T], axis=1)
    paired = sizes["fsdp"] == 4 and ctx == 2 and group == 1 and bits_of(tp)
    if paired:
        x_all16, qkvo, both_ff = opening(
            tokens, shard, jnp.pad(jnp.stack([w_first, w_second.T]), ((0, 0), (0, 0), (0, padding))), tp
        )
        both_ff = both_ff.reshape(2, tp, width, units + padding)
        x_all16 = x_all16.reshape(2 * rows * span, width)
    else:
        first = lax.all_gather(w_first, both, axis=0, tiled=True).reshape(tp, width, units)
        second = lax.all_gather(w_second.T, both, axis=0, tiled=True).reshape(tp, width, units)
        qkvo = lax.all_gather(shard, both, axis=0, tiled=True).reshape(tp, width, 4, heads_dev)
        qkvo = qkvo.transpose(2, 0, 3, 1).reshape(4, tp * heads_dev, width)
        x16 = jnp.concatenate(gather_row(tokens), axis=0)
        x_all16 = jnp.concatenate([x16] + [fetch(x16, i) for i in range(1, steps)], axis=0)
    wq, wkv, wo = qkvo[0], qkvo[1:3].reshape(2 * tp * heads_dev, width), qkvo[3]
    count = rows * span
    ids = lax.dynamic_index_in_dim(picture, row, 0, keepdims=False).reshape(tp, span)
    if not paired:
        order = part * rows + (row - jnp.arange(rows)) % rows
        ids = jnp.take(ids, order, axis=0)
    ids = ids.reshape(count)
    cotangent, x_all16 = lax.optimization_barrier((cotangent, x_all16))
    cot = gather_row(cotangent)
    if paired:
        cot = in_order(cot)
    else:
        cot = jnp.concatenate(cot, axis=0)
    kid = jnp.concatenate([ids] + [fetch(ids, i) for i in range(1, steps)], axis=0)
    block = 256 if count % 256 == 0 else count
    blocks, index = active_blocks(ids, kid, block, block)
    numbers = jnp.arange(8)[:, None]
    qm = jnp.where((numbers < PICS) & (ids[None, :] != numbers), NEG, 0.0).astype(F32)
    km = (kid[None, :] == numbers).astype(F32)

    x_all = x_all16.astype(F32)
    scaled_all, inverse_all = norm_stats(x_all)
    n1 = (scaled_all * ln1_gain + ln1_bias).astype(BF16)
    qt = ((dot(wq, n1[:count], 1, 1) + b_query[:, None]) * (HD ** (-0.5) * LOG2E)).astype(BF16)
    kv_bias = jnp.concatenate([jnp.zeros_like(b_value), b_value])
    kvt = (dot(wkv, n1, 1, 1) + kv_bias[:, None]).astype(BF16)
    ot, lse = attention_forward(blocks, index, qt, kvt, qm, km, block)
    h = x_all[:count] + (dot(ot, wo, 0, 0) + b_output)

    scaled2, inverse2 = norm_stats(h)
    n2 = (scaled2 * ln2_gain + ln2_bias).astype(BF16)
    if paired:
        y, d_n2, g_first, g_second, g_bf = feed(
            n2, cot, jnp.pad(b_first.reshape(tp, 1, units), ((0, 0), (0, 0), (0, padding))), both_ff, tp
        )
        g_first, g_second = g_first[:, :units], g_second[:, :units]
        g_bf = g_bf[:, :, :units].reshape(-1)
        y = h + b_second + y
    else:
        y = h + b_second
        d_n2 = jnp.zeros_like(h)
        g_first, g_second, g_first_bias = [], [], []
        for t in range(tp):
            pre = dot(n2, first[t], 1, 0) + b_first[t * units : (t + 1) * units]
            value, slope = gelu_pair(pre)
            act = value.astype(BF16)
            y = y + dot(act, second[t], 1, 1)
            d_pre = (dot(cot, second[t], 1, 0) * slope).astype(BF16)
            d_n2 = d_n2 + dot(d_pre, first[t], 1, 1)
            g_second.append(dot(cot, act, 0, 0).astype(BF16))
            g_first.append(dot(n2, d_pre, 0, 0).astype(BF16))
            g_first_bias.append(jnp.sum(d_pre.astype(F32), axis=0))
        g_bf = jnp.concatenate(g_first_bias)
    output = y.astype(BF16)
    if paired:
        output = output.reshape(rows, span, width)
        output = scatter_row([lax.dynamic_index_in_dim(output, (place - k) % rows, 0, False) for k in range(rows)])
    else:
        output = scatter_row([output[k * span : (k + 1) * span] for k in range(rows)])
    cot32 = cot.astype(F32)
    g_g2 = jnp.sum(d_n2 * scaled2, axis=0)
    g_c2 = jnp.sum(d_n2, axis=0)
    d_h = cot32 + norm_back(d_n2, scaled2, inverse2, ln2_gain)
    g_bs = jnp.sum(cot32, axis=0)

    d_att = d_h.astype(BF16)
    g_bo = jnp.sum(d_att.astype(F32), axis=0)
    d_ot = dot(wo, d_att, 1, 1).astype(BF16)
    dqt, dkt, dvt = attention_backward(blocks, index, qt, kvt, d_ot, ot, lse, qm, km, block)
    wk, wv = wkv[: tp * heads_dev], wkv[tp * heads_dev :]
    g_bq = jnp.sum(dqt.astype(F32), axis=1)
    g_bv = jnp.sum(dvt.astype(F32), axis=1)
    scaled1, inverse1 = scaled_all[:count], inverse_all[:count]

    def pack(parts):
        vector = jnp.concatenate(parts)
        return jnp.pad(vector, (0, -vector.shape[0] % 1024)).reshape(-1, 128)

    small = [g_bq, g_bv, g_bo, g_g2, g_c2, g_bf, g_bs]
    if paired:
        d_other = (dot(dkt[:, count:], wk, 0, 0) + dot(dvt[:, count:], wv, 0, 0)).astype(BF16)
        d_own = dot(dkt[:, :count], wk, 0, 0) + dot(dvt[:, :count], wv, 0, 0) + dot(dqt, wq, 0, 0)
        free = [jnp.zeros((2 * width,), F32)]
        g_query, g_key, g_value, g_out, vector, grad_tokens = closing(
            d_other, d_own, d_h, x_all16[:count], n1, d_att, ln1_gain[None, :], dqt, dkt, dvt, ot,
            pack(free + small), tp,
        )
    else:
        d_all = dot(dkt, wk, 0, 0) + dot(dvt, wv, 0, 0)
        d_n1 = d_all[:count] + dot(dqt, wq, 0, 0)
        for i in range(1, steps):
            d_n1 = d_n1 + give(d_all[i * count : (i + 1) * count].astype(BF16), i).astype(F32)
        head_grads = [dot(n1[:count], dqt, 0, 1), dot(n1, dkt, 0, 1), dot(n1, dvt, 0, 1), dot(d_att, ot, 0, 1)]
        g_first, g_second = (
            scatter_units([halve(g, sizes, i % 2 == 0) for g in parts], tp)
            for i, parts in enumerate((g_first, g_second))
        )
        halved = [halve(g.astype(BF16), sizes, i % 2 == 0) for i, g in enumerate(head_grads)]
        g_query, g_key, g_value, g_out = (
            scatter_units([g[:, t * heads_dev : (t + 1) * heads_dev] for t in range(tp)], tp) for g in halved
        )
        vector = butterfly(pack([jnp.sum(d_n1 * scaled1, axis=0), jnp.sum(d_n1, axis=0)] + small), sizes)
        grad_tokens = (d_h + norm_back(d_n1, scaled1, inverse1, ln1_gain)).astype(BF16)
        grad_tokens = scatter_row([grad_tokens[k * span : (k + 1) * span] for k in range(rows)])
    grad_tokens = grad_tokens.astype(F32)
    g_out, g_second = g_out.T, g_second.T
    vector = vector.reshape(-1)
    lengths = [width, width] + [p.shape[0] for p in small]
    ends = [sum(lengths[:i]) for i in range(len(lengths) + 1)]
    g_g1, g_c1, g_bq, g_bv, g_bo, g_g2, g_c2, g_bf, g_bs = (vector[i:j] for i, j in zip(ends, ends[1:]))
    return (
        output, grad_tokens, g_g1, g_c1, g_query, g_bq, g_key, g_value, g_bv, g_out, g_bo,
        g_g2, g_c2, g_first, g_bf, g_second, g_bs,
    )


def solution(mesh):
    rows_spec = P("fsdp", ("ctx", "tp"), None)
    column, line = P("fsdp", "tp"), P("tp", "fsdp")
    column_out, line_out = P(("fsdp", "ctx"), "tp"), P("tp", ("fsdp", "ctx"))
    return jax.shard_map(
        functools.partial(shards, dict(mesh.shape)),
        mesh=mesh,
        in_specs=(
            rows_spec, P("fsdp", "ctx"), P(), P(), column, P(), column, column, P(), line, P(),
            P(), P(), column, P(), line, P(), rows_spec,
        ),
        out_specs=(
            rows_spec, rows_spec, P(), P(), column_out, P(), column_out, column_out, P(), line_out,
            P(), P(), P(), column_out, P(), line_out, P(),
        ),
        check_vma=False,
    )
```
